32 devices in a mesh: groups: 2 (over y), vocab: 4 (over z), edit: 2 (over x), tok: 2 (over core).
Axes of the slice: x: 2, y: 2, z: 4, core: 2. Of those that a mesh axis runs over, the one named last changes fastest.
Arguments:
- token_ids: int32 [256], P(('groups', 'tok')), parts along dimension 0, may hold values from 0 to 4095
- valid_mask: int32 [256], P(('groups', 'tok')), parts along dimension 0, may hold values 0 or 1
- key_index: int32 [4], P('groups'), parts along dimension 0, may hold values from 0 to 3
- hidden_act: bfloat16 [256, 14336], P(('groups', 'tok'), 'vocab'), parts along dimension 0, may hold values from -6 to 6
- key_table: bfloat16 [4, 14336], P(None, 'vocab'), may hold values from -0.046875 to 0.046875
- base_out: bfloat16 [256, 4096], P(('groups', 'tok'), 'vocab'), parts along dimension 0, may hold values from -50 to 50
- value_vecs: bfloat16 [4, 4096], P(('groups', 'edit'), 'vocab'), parts along dimension 0, may hold values from -6 to 6
- norm_gain: float32 [4096], replicated, may hold values from 0.5 to 1.5
- head: bfloat16 [4096, 4096], P(('vocab', 'edit')), may hold values from -46 to 46
Outputs:
- grad_value: float32 [4, 4096], P(('groups', 'edit'), 'vocab'), parts along dimension 0
- token_kl: float32 [4, 128], P(('groups', 'edit'), 'tok'), parts along dimension 0
- target_logprob: float32 [4, 128], P(('groups', 'edit'), 'tok'), parts along dimension 0
The draws below stay inside these ranges and needn't reach their ends.
There are 2 independent parts, one for each index of `groups`. The reference program is written for one: setup_inputs(seed, part) draws one part's arguments, and reference() takes and returns one part's arrays. A program takes and returns all parts, laid end to end along the dimension named above; an argument that names none is the same for every part. Nothing has to cross between parts.
All inputs are finite; a program needn't handle non-finite values. No bound on the sum of `valid_mask` on one device may be relied on, other than what follows from the above.
Results may differ from the reference program's by a relative error of at most 0.0061.
Values may be sent and summed in bfloat16 or wider, within the bound.
A program may use at most 64 MiB of HBM per device.

```python
import math
import jax
import jax.numpy as jnp
import numpy as np
from jax import lax

D = 4096
FF = 14336
VOCAB = 4096
EDITS = 2
TOKENS = 128
KEYS = 4


def draw_base_out(key, part):
    key_a = jax.random.fold_in(key, 101)
    key_b = jax.random.fold_in(key, 102)
    key_c = jax.random.fold_in(key, 103)
    noise_part = jnp.clip(jax.random.normal(key_a, (TOKENS, D), jnp.float32), -4.0, 4.0)
    row_scale = jnp.exp(jax.random.uniform(key_b, (TOKENS, 1), jnp.float32, 0.0, math.log(10.0))) / 3.0
    col_scale = jnp.exp(jax.random.uniform(key_c, (1, D), jnp.float32, math.log(0.5), math.log(2.0)))
    return (noise_part * row_scale * col_scale).astype(jnp.bfloat16)


def draw_head(key, part):
    key_a = jax.random.fold_in(key, 201)
    spread = 3.0 / math.sqrt(D)
    drawn_rows = jnp.clip(jax.random.normal(key_a, (VOCAB, D), jnp.float32), -4.0, 4.0) * spread
    return drawn_rows.astype(jnp.bfloat16)


def touch_ends(values, stream_key, least, largest):
    dims = values.shape
    index_at = [jax.random.randint(jax.random.fold_in(stream_key, axis), (), 0, dims[axis]) for axis in range(len(dims))]
    values = values.at[tuple(index_at)].set(least)
    longest = dims.index(max(dims))
    index_at[longest] = (index_at[longest] + 1) % dims[longest]
    return values.at[tuple(index_at)].set(largest)


def level_of(rng, extent, cuts, smallest, top_value):
    def one(dim, blocks):
        steps = jax.random.uniform(jax.random.fold_in(jax.random.fold_in(rng, 6), dim), (blocks,), jnp.float32, smallest / len(cuts), top_value / len(cuts))
        return jnp.repeat(jnp.exp(steps), extent[dim] // blocks).reshape((-1,) + (1,) * (len(extent) - dim - 1))

    level = one(*cuts[0])
    for cut in cuts[1:]:
        level = level * one(*cut)
    return level


def rank_table(amount, slope):
    weights = [(1 << 20) // math.isqrt(standing ** slope) + 1 for standing in range(1, amount + 1)]
    deviation = 1 + sum(weights) // (1 << 30)
    return np.cumsum(np.array([max(1, weight // deviation) for weight in weights]))


def skewed_ids(own_key, shape, amount, slope):
    table = rank_table(amount, slope)
    pick = jax.random.randint(jax.random.fold_in(own_key, 1), shape, 0, int(table[amount - 1]))
    rank = jnp.searchsorted(jnp.asarray(table, jnp.int32), pick, side="right")
    return jax.random.permutation(jax.random.fold_in(own_key, 2), amount)[rank].astype(jnp.int32)


def bell_draw(rng, shape, width, most, shards=(), kind=jnp.bfloat16):
    gain = level_of(rng, shape, shards, -0.22, 0.18) if shards else 1.0
    entries = jax.random.normal(rng, shape, jnp.float32) * width * gain
    return jnp.minimum(jnp.maximum(entries, -most), most).astype(kind)


def setup_inputs(seed: int = 0, part: int = 0) -> dict:
    seeds = jax.random.split(jax.random.key(seed), 10)
    part_splits = jax.random.split(jax.random.fold_in(seeds[9], part), 10)
    token_ids = touch_ends(skewed_ids(part_splits[0], (TOKENS,), VOCAB, 2), jax.random.fold_in(part_splits[0], 3), 0, VOCAB - 1).astype(jnp.int32)
    valid_mask = touch_ends((jax.random.randint(part_splits[1], (TOKENS,), 0, 4) < 3).astype(jnp.int32), jax.random.fold_in(part_splits[1], 1), 0, 1)
    key_index = jax.random.randint(part_splits[2], (EDITS,), 0, KEYS).astype(jnp.int32)
    hidden_act = bell_draw(part_splits[3], (TOKENS, FF), 1.0, 6.0, ((0, 2), (1, 4)))
    key_table = bell_draw(seeds[4], (KEYS, FF), FF ** -0.5, 0.046875, ((1, 4),))
    base_out = draw_base_out(jax.random.fold_in(jax.random.fold_in(seeds[9], part), 71), part)
    value_vecs = bell_draw(part_splits[6], (EDITS, D), 1.0, 6.0, ((0, 2), (1, 4)))
    norm_gain = jnp.clip(1.0 + 0.1 * jax.random.normal(seeds[7], (D,), jnp.float32), 0.5, 1.5)
    head = draw_head(jax.random.fold_in(seeds[9], 71), part)
    return dict(token_ids=token_ids, valid_mask=valid_mask, key_index=key_index, hidden_act=hidden_act, key_table=key_table, base_out=base_out, value_vecs=value_vecs, norm_gain=norm_gain, head=head)


NORM_EPS = 1e-05

def rms_scale(hidden_rows):
    return lax.rsqrt(lax.optimization_barrier(jnp.mean(hidden_rows * hidden_rows, axis=-1, keepdims=True)) + NORM_EPS)

def log_total(logit_rows):
    peak_value = lax.optimization_barrier(jnp.max(logit_rows, axis=-1, keepdims=True))
    return peak_value[..., 0] + jnp.log(lax.optimization_barrier(jnp.sum(jnp.exp(logit_rows - peak_value), axis=-1)))

def reference(token_ids, valid_mask, key_index, hidden_act, key_table, base_out, value_vecs, norm_gain, head):
    edit_keys = key_table[key_index.astype(jnp.int32)]
    coeff = jnp.dot(edit_keys, hidden_act.T, preferred_element_type=jnp.float32)
    base32 = base_out.astype(jnp.float32)
    base_norm = (norm_gain * base32 * rms_scale(base32)).astype(jnp.bfloat16)
    base_logits = jnp.dot(base_norm, head.T, preferred_element_type=jnp.float32)
    base_lse = log_total(base_logits)
    base_prob = jnp.exp(base_logits - base_lse[:, None])
    valid = valid_mask.astype(jnp.float32)
    vocab_ids = jnp.arange(head.shape[0], dtype=jnp.int32)
    onehot = (token_ids.astype(jnp.int32)[:, None] == vocab_ids[None, :]).astype(jnp.float32)

    def one_edit(edit_args):
        row_coeff, value_row = edit_args
        edited = base32 + row_coeff[:, None] * value_row.astype(jnp.float32)[None, :]
        row_scale = rms_scale(edited)
        normed = (norm_gain * edited * row_scale).astype(jnp.bfloat16)
        logits = jnp.dot(normed, head.T, preferred_element_type=jnp.float32)
        edit_lse = log_total(logits)
        kl_rows = valid * (lax.optimization_barrier(jnp.sum(base_prob * (base_logits - logits), axis=-1)) - base_lse + edit_lse)
        target_rows = lax.optimization_barrier(jnp.sum(onehot * logits, axis=-1)) - edit_lse
        logit_grad = (valid[:, None] * (jnp.exp(logits - edit_lse[:, None]) - base_prob)).astype(jnp.bfloat16)
        back_rows = jnp.dot(logit_grad, head, preferred_element_type=jnp.float32)
        grad_y = norm_gain * back_rows
        grad_o = row_scale * grad_y - edited * row_scale ** 3 * lax.optimization_barrier(jnp.mean(grad_y * edited, axis=-1, keepdims=True))
        grad_row = lax.optimization_barrier(jnp.sum(row_coeff[:, None] * grad_o, axis=0))
        return (kl_rows, target_rows, grad_row)
    token_kl, target_logprob, grad_value = lax.map(one_edit, (coeff, value_vecs))
    return (grad_value, token_kl, target_logprob)
```

```python
import functools

import jax
import jax.numpy as jnp
from jax import lax
from jax.experimental import pallas as pl
from jax.experimental.pallas import tpu as pltpu
from jax.sharding import PartitionSpec as P

NORM_EPS = 1e-05


def rms_scale(hidden_rows):
    return lax.rsqrt(jnp.mean(hidden_rows * hidden_rows, axis=-1, keepdims=True) + NORM_EPS)


def per_device(
    token_ids, valid_mask, key_index, hidden_act, key_table, base_out, value_vecs, norm_gain, head
):
    vocab_rows = head.shape[0]
    edit_rows = value_vecs.shape[0]
    piece_width = value_vecs.shape[1]
    key_slots = jnp.arange(key_table.shape[0], dtype=jnp.int32)
    select = (key_index[:, None] == key_slots[None, :]).astype(jnp.bfloat16)
    edit_keys = jnp.dot(select, key_table, preferred_element_type=jnp.float32).astype(jnp.bfloat16)
    coeff_part = lax.dot_general(
        edit_keys, hidden_act, (((1,), (1,)), ((), ())), preferred_element_type=jnp.float32
    )
    coeff = lax.psum(coeff_part, "vocab")
    base_rows, local_values = (
        lax.all_gather(base_out, "vocab", axis=1, tiled=True),
        lax.all_gather(value_vecs, "vocab", axis=1, tiled=True),
    )
    values = lax.all_gather(local_values, "edit", axis=0, tiled=True)
    base32 = base_rows.astype(jnp.float32)
    base_norm = (norm_gain * base32 * rms_scale(base32)).astype(jnp.bfloat16)
    base_logits = lax.dot_general(
        base_norm, head, (((1,), (1,)), ((), ())), preferred_element_type=jnp.float32
    )
    edited = base32[None, :, :] + coeff[:, :, None] * values.astype(jnp.float32)[:, None, :]
    row_scale = rms_scale(edited)
    normed = (norm_gain * edited * row_scale).astype(jnp.bfloat16)
    logits = jnp.einsum("etd,vd->etv", normed, head, preferred_element_type=jnp.float32)
    vocab_start = lax.axis_index(("vocab", "edit")) * vocab_rows
    vocab_ids = vocab_start + jnp.arange(vocab_rows, dtype=jnp.int32)
    onehot = (token_ids[:, None] == vocab_ids[None, :]).astype(jnp.float32)
    peak_base = jnp.max(base_logits, axis=-1)
    peak_edit = jnp.max(logits, axis=-1)
    peak_base, peak_edit = lax.pmax((peak_base, peak_edit), ("vocab", "edit"))
    base_exp = jnp.exp(base_logits - peak_base[:, None])
    base_total = jnp.sum(base_exp, axis=-1)
    edit_total = jnp.sum(jnp.exp(logits - peak_edit[:, :, None]), axis=-1)
    cross_sum = jnp.sum(base_exp[None, :, :] * (base_logits[None, :, :] - logits), axis=-1)
    target = jnp.sum(onehot[None, :, :] * logits, axis=-1)
    base_total, edit_total, cross_sum, target = lax.psum(
        (base_total, edit_total, cross_sum, target), ("vocab", "edit")
    )
    base_lse = peak_base + jnp.log(base_total)
    edit_lse = peak_edit + jnp.log(edit_total)
    valid = valid_mask.astype(jnp.float32)
    token_kl = valid[None, :] * (cross_sum / base_total[None, :] - base_lse[None, :] + edit_lse)
    target_logprob = target - edit_lse
    base_prob = jnp.exp(base_logits - base_lse[:, None])
    edit_prob = jnp.exp(logits - edit_lse[:, :, None])
    logit_grad = (valid[None, :, None] * (edit_prob - base_prob[None, :, :])).astype(jnp.bfloat16)
    back_rows = jnp.einsum("etv,vd->etd", logit_grad, head, preferred_element_type=jnp.float32)
    grad_y = norm_gain * back_rows
    grad_o = row_scale * grad_y - edited * row_scale**3 * jnp.mean(
        grad_y * edited, axis=-1, keepdims=True
    )
    grad_part = jnp.sum(coeff[:, :, None] * grad_o, axis=1)
    edit_start = lax.axis_index("edit") * edit_rows
    grad_total = lax.psum(grad_part, ("vocab", "edit", "tok"))
    grad_mine = lax.dynamic_slice_in_dim(grad_total, edit_start, edit_rows, 0)
    grad_piece = lax.dynamic_slice_in_dim(
        grad_mine, lax.axis_index("vocab") * piece_width, piece_width, 1
    )
    kl_mine = lax.dynamic_slice_in_dim(token_kl, edit_start, edit_rows, 0)
    target_mine = lax.dynamic_slice_in_dim(target_logprob, edit_start, edit_rows, 0)
    return (grad_piece, kl_mine, target_mine)


MESH = pl.DeviceIdType.MESH


def split_rows(row, where_mask):
    hi = row.astype(jnp.bfloat16).astype(jnp.float32)
    rest = row - hi
    mid = rest.astype(jnp.bfloat16).astype(jnp.float32)
    low = rest - mid
    at = lax.broadcasted_iota(jnp.int32, (8, row.shape[1]), 0)
    rows = jnp.where(at == 0, hi, jnp.where(at == 1, mid, jnp.where(at == 2, low, 0.0)))
    return rows if where_mask is None else jnp.where(where_mask, rows, 0.0)


def fused(
    nv,
    key_ref,
    ids_ref,
    mask_ref,
    act_hbm,
    table_ref,
    base_hbm,
    val_ref,
    gain_ref,
    head_hbm,
    grad_ref,
    kl_ref,
    tl_ref,
    act,
    head,
    rows_all,
    vals,
    myval,
    cpart,
    call,
    normed,
    stat,
    stats,
    wmine,
    wother,
    smine,
    sother,
    gpart,
    gall,
    local_sem,
    head_sem,
    zs,
    zr,
    xs,
    xr,
    vs,
    vr,
    cs,
    cr,
    ss,
    sr,
    gs,
    gr,
    ts,
    tr,
):
    f32, bf16 = jnp.float32, jnp.bfloat16
    z = lax.axis_index("vocab")
    x = lax.axis_index("edit")
    c = lax.axis_index("tok")
    q = z * 2 + x
    nq = nv * 2
    tk, width = base_hbm.shape
    half = tk // 2
    dim = gain_ref.shape[1]
    vrows = head_hbm.shape[0]
    hv = vrows // 4

    barrier = pltpu.get_barrier_semaphore()
    peers = []
    for k in range(1, nq):
        p = lax.rem(q + k, nq)
        peers.append({"vocab": p // 2, "edit": lax.rem(p, 2)})
    buddy = {"tok": 1 - c}
    for p in peers:
        pl.semaphore_signal(barrier, inc=1, device_id=p, device_id_type=MESH)
    pl.semaphore_signal(barrier, inc=1, device_id=buddy, device_id_type=MESH)

    base_in = pltpu.make_async_copy(base_hbm, rows_all.at[z], local_sem.at[0])
    base_in.start()
    act_in = pltpu.make_async_copy(act_hbm, act, local_sem.at[1])
    act_in.start()
    head_in = [
        pltpu.make_async_copy(
            head_hbm.at[pl.ds(i * hv, hv)], head.at[pl.ds(i * hv, hv)], head_sem.at[i]
        )
        for i in range(4)
    ]
    for d in head_in:
        d.start()
    myval[...] = val_ref[...].astype(f32)
    vals[x, z] = myval[...]
    base_in.wait()
    pl.semaphore_wait(barrier, nq)

    mine = pl.ds(pl.multiple_of(x * half, half), half)

    def send(src, dst, ssem, rsem, dev):
        d = pltpu.make_async_remote_copy(
            src_ref=src, dst_ref=dst, send_sem=ssem, recv_sem=rsem, device_id=dev, device_id_type=MESH
        )
        d.start()
        return d

    order = [1, nv - 1] + [k for k in range(2, nv - 1)]
    zcopies = {}
    for k in order:
        zcopies[k] = send(
            rows_all.at[z, mine], rows_all.at[z, mine], zs.at[k], zr.at[k], {"vocab": lax.rem(z + k, nv)}
        )
    vcopies = [
        send(myval, vals.at[x, z], vs.at[k], vr.at[k], peers[k]) for k in range(nq - 1)
    ]

    act_in.wait()
    every = lax.dot_general(
        table_ref[...], act[...], (((1,), (1,)), ((), ())), preferred_element_type=f32
    )
    picked = []
    for e in range(2):
        one = jnp.zeros((1, tk), f32)
        for k in range(every.shape[0]):
            one = one + jnp.where(key_ref[e] == k, every[k : k + 1, :], 0.0)
        picked.append(one)
    for e in range(2):
        cpart[e] = picked[e]
    call[z] = cpart[...]
    ccopies = [
        send(cpart, call.at[z], cs.at[k], cr.at[k], {"vocab": lax.rem(z + k, nv)})
        for k in range(1, nv)
    ]

    sub = lax.broadcasted_iota(jnp.int32, (tk, 2 * tk), 0)
    lane = lax.broadcasted_iota(jnp.int32, (tk, 2 * tk), 1)
    first = lane < tk
    diag = jnp.where(first, lane, lane - tk) == sub
    eye = lax.broadcasted_iota(jnp.int32, (tk, tk), 0) == lax.broadcasted_iota(
        jnp.int32, (tk, tk), 1
    )

    def to_col(row):
        return jnp.sum(jnp.where(eye, row, 0.0), axis=1, keepdims=True)

    def to_row(col0, col1):
        return jnp.sum(
            jnp.where(diag, jnp.where(first, col0, col1), 0.0), axis=0, keepdims=True
        )

    ids_col = to_col(ids_ref[...].astype(f32))
    ids_row = to_row(ids_col, ids_col)
    valid_col = to_col(mask_ref[...].astype(f32))
    valid = to_row(valid_col, valid_col)

    xcopies = []
    for k in order:
        zcopies[k].wait_recv()
        s = lax.rem(z - k + nv, nv)
        xcopies.append(
            send(
                rows_all.at[s, mine], rows_all.at[s, mine], xs.at[k], xr.at[k], {"edit": 1 - x}
            )
        )
    for d in ccopies:
        d.wait_recv()
    for d in vcopies:
        d.wait_recv()
    coeff = []
    for e in range(2):
        total = call[0, e]
        for s in range(1, nv):
            total = total + call[s, e]
        coeff.append(to_col(total))
    for d in xcopies:
        d.wait_recv()

    sq = [jnp.zeros((tk, 1), f32) for _ in range(3)]
    for s in range(nv):
        b = rows_all[s].astype(f32)
        sq[0] = sq[0] + jnp.sum(b * b, axis=1, keepdims=True)
        for e in range(2):
            ed = b + coeff[e] * vals[e, s]
            sq[1 + e] = sq[1 + e] + jnp.sum(ed * ed, axis=1, keepdims=True)
    scale = [lax.rsqrt(t / dim + NORM_EPS) for t in sq]
    for s in range(nv):
        cols = pl.ds(s * width, width)
        b = rows_all[s].astype(f32)
        gain = gain_ref[:, cols]
        plain = (gain * b * scale[0]).astype(bf16)
        normed[0:tk, cols] = plain
        normed[tk : 2 * tk, cols] = plain
        for e in range(2):
            ed = b + coeff[e] * vals[e, s]
            normed[(2 + e) * tk : (3 + e) * tk, cols] = (gain * ed * scale[1 + e]).astype(bf16)
    for d in head_in:
        d.wait()
    logit = lax.dot_general(
        head[...], normed[...], (((1,), (1,)), ((), ())), preferred_element_type=f32
    )
    lb, le = logit[:, : 2 * tk], logit[:, 2 * tk :]
    vid = (q * vrows + lax.broadcasted_iota(jnp.int32, lb.shape, 0)).astype(f32)
    mb = jnp.max(lb, axis=0, keepdims=True)
    me = jnp.max(le, axis=0, keepdims=True)
    eb = jnp.exp(lb - mb)
    ee = jnp.exp(le - me)
    stat[0:1] = mb
    stat[1:2] = me
    stat[2:3] = jnp.sum(eb, axis=0, keepdims=True)
    stat[3:4] = jnp.sum(ee, axis=0, keepdims=True)
    stat[4:5] = jnp.sum(eb * (lb - le), axis=0, keepdims=True)
    stat[5:6] = jnp.sum(eb * le, axis=0, keepdims=True)
    stat[6:7] = jnp.sum(ee * le, axis=0, keepdims=True)
    stat[7:8] = jnp.sum(jnp.where(vid == ids_row, le, 0.0), axis=0, keepdims=True)
    stats[q] = stat[...]
    scopies = [send(stat, stats.at[q], ss.at[k], sr.at[k], peers[k]) for k in range(nq - 1)]
    cr_row = to_row(coeff[0] * scale[1], coeff[1] * scale[2])
    crr_row = to_row(coeff[0] * scale[1] * scale[1], coeff[1] * scale[2] * scale[2])
    lanes8 = lax.broadcasted_iota(jnp.int32, (8, 2 * tk), 1)
    lhs = jnp.concatenate(
        [split_rows(cr_row, lanes8 < tk), split_rows(cr_row, lanes8 >= tk)], axis=0
    ).astype(bf16)
    for d in scopies:
        d.wait_recv()

    pb, pe = stats[0, 0:1], stats[0, 1:2]
    for p in range(1, nq):
        pb = jnp.maximum(pb, stats[p, 0:1])
        pe = jnp.maximum(pe, stats[p, 1:2])
    sums = [jnp.zeros((1, 2 * tk), f32) for _ in range(6)]
    for p in range(nq):
        fb = jnp.exp(stats[p, 0:1] - pb)
        fe = jnp.exp(stats[p, 1:2] - pe)
        for j, f in enumerate((fb, fe, fb, fb, fe, None)):
            got = stats[p, 2 + j : 3 + j]
            sums[j] = sums[j] + (got if f is None else f * got)
    tb, te, cross, meanb, meane, target = sums
    lse_b = pb + jnp.log(tb)
    lse_e = pe + jnp.log(te)
    lg = (valid * (jnp.exp(le - lse_e) - jnp.exp(lb - lse_b))).astype(bf16)
    w = lax.dot_general(lhs, lg, (((1,), (1,)), ((), ())), preferred_element_type=f32)
    wmine[0] = jnp.sum(w[0:8], axis=0, keepdims=True)
    wmine[1] = jnp.sum(w[8:16], axis=0, keepdims=True)
    wcopy = send(wmine, wother, ts.at[0], tr.at[0], buddy)

    pull = crr_row * valid * (meane / te - meanb / tb) / dim
    own = lane - tk * x == sub
    pull_col = jnp.sum(jnp.where(own, pull, 0.0), axis=1, keepdims=True)
    own_coeff = jnp.where(x == 0, coeff[0], coeff[1])
    ed = rows_all[z].astype(f32) + own_coeff * myval[...]
    smine[...] = jnp.sum(pull_col * ed, axis=0, keepdims=True)
    scopy = send(smine, sother, ts.at[1], tr.at[1], buddy)
    kl = valid * (cross / tb - lse_b + lse_e)
    tl = target - lse_e
    kl_ref[...] = jnp.where(x == 0, kl, pltpu.roll(kl, tk, 1))[:, :tk]
    tl_ref[...] = jnp.where(x == 0, tl, pltpu.roll(tl, tk, 1))[:, :tk]

    wcopy.wait_recv()
    wl = jnp.concatenate(
        [split_rows(wmine[e] + wother[e], None) for e in range(2)], axis=0
    ).astype(bf16)
    back = lax.dot_general(wl, head[...], (((1,), (0,)), ((), ())), preferred_element_type=f32)
    for e in range(2):
        g = jnp.sum(back[e * 8 : e * 8 + 8], axis=0, keepdims=True) * gain_ref[...]
        for s in range(nv):
            gpart[e, s] = g[:, s * width : (s + 1) * width]
    gall[q] = gpart[x, z]
    gcopies = []
    for k in range(nq - 1):
        p = peers[k]
        gcopies.append(send(gpart.at[p["edit"], p["vocab"]], gall.at[q], gs.at[k], gr.at[k], p))
    scopy.wait_recv()
    out = -(smine[...] + sother[...])
    for d in gcopies:
        d.wait_recv()
    for p in range(nq):
        out = out + gall[p]
    grad_ref[...] = out
    for d in list(zcopies.values()) + vcopies + ccopies + xcopies + scopies + gcopies:
        d.wait_send()
    wcopy.wait_send()
    scopy.wait_send()


def kernel_device(
    nv, token_ids, valid_mask, key_index, hidden_act, key_table, base_out, value_vecs, norm_gain, head
):
    f32, bf16 = jnp.float32, jnp.bfloat16
    tk, width = base_out.shape
    dim = head.shape[1]
    vrows = head.shape[0]
    nq = nv * 2
    dma = lambda n: pltpu.SemaphoreType.DMA((n,))
    vmem = pl.BlockSpec(memory_space=pltpu.VMEM)
    hbm = pl.BlockSpec(memory_space=pl.ANY)
    smem = pl.BlockSpec(memory_space=pltpu.SMEM)
    return pl.pallas_call(
        functools.partial(fused, nv),
        out_shape=(
            jax.ShapeDtypeStruct((1, width), f32),
            jax.ShapeDtypeStruct((1, tk), f32),
            jax.ShapeDtypeStruct((1, tk), f32),
        ),
        in_specs=[smem, vmem, vmem, hbm, vmem, hbm, vmem, vmem, hbm],
        out_specs=(vmem, vmem, vmem),
        scratch_shapes=[
            pltpu.VMEM(hidden_act.shape, bf16),
            pltpu.VMEM(head.shape, bf16),
            pltpu.VMEM((nv, tk, width), bf16),
            pltpu.VMEM((2, nv, 1, width), f32),
            pltpu.VMEM((1, width), f32),
            pltpu.VMEM((2, 1, tk), f32),
            pltpu.VMEM((nv, 2, 1, tk), f32),
            pltpu.VMEM((4 * tk, dim), bf16),
            pltpu.VMEM((8, 2 * tk), f32),
            pltpu.VMEM((nq, 8, 2 * tk), f32),
            pltpu.VMEM((2, 1, vrows), f32),
            pltpu.VMEM((2, 1, vrows), f32),
            pltpu.VMEM((1, width), f32),
            pltpu.VMEM((1, width), f32),
            pltpu.VMEM((2, nv, 1, width), f32),
            pltpu.VMEM((nq, 1, width), f32),
            dma(2), dma(4),
            dma(nv), dma(nv), dma(nv), dma(nv),
            dma(nq), dma(nq), dma(nv), dma(nv),
            dma(nq), dma(nq), dma(nq), dma(nq),
            dma(2), dma(2),
        ],
        compiler_params=pltpu.CompilerParams(
            collective_id=0, has_side_effects=True, vmem_limit_bytes=48 * 1024 * 1024
        ),
    )(
        key_index,
        token_ids.reshape(1, tk),
        valid_mask.reshape(1, tk),
        hidden_act,
        key_table,
        base_out,
        value_vecs,
        norm_gain.reshape(1, dim),
        head,
    )


def solution(mesh):
    placed = (
        P(("groups", "tok")),
        P(("groups", "tok")),
        P("groups"),
        P(("groups", "tok"), "vocab"),
        P(None, "vocab"),
        P(("groups", "tok"), "vocab"),
        P(("groups", "edit"), "vocab"),
        P(),
        P(("vocab", "edit"), None),
    )
    body = per_device
    if mesh.shape["edit"] == 2 and mesh.shape["tok"] == 2 and 3 <= mesh.shape["vocab"] <= 4:
        body = functools.partial(kernel_device, mesh.shape["vocab"])
    return jax.shard_map(
        body,
        mesh=mesh,
        in_specs=placed,
        out_specs=(
            P(("groups", "edit"), "vocab"),
            P(("groups", "edit"), "tok"),
            P(("groups", "edit"), "tok"),
        ),
        check_vma=False,
    )
```

```python
import functools

import jax
import jax.numpy as jnp
from jax import lax
from jax.experimental import pallas as pl
from jax.experimental.pallas import tpu as pltpu
from jax.sharding import PartitionSpec as P

NORM_EPS = 1e-05


def rms_scale(hidden_rows):
    return lax.rsqrt(jnp.mean(hidden_rows * hidden_rows, axis=-1, keepdims=True) + NORM_EPS)


def per_device(
    token_ids, valid_mask, key_index, hidden_act, key_table, base_out, value_vecs, norm_gain, head
):
    vocab_rows = head.shape[0]
    edit_rows = value_vecs.shape[0]
    piece_width = value_vecs.shape[1]
    key_slots = jnp.arange(key_table.shape[0], dtype=jnp.int32)
    select = (key_index[:, None] == key_slots[None, :]).astype(jnp.bfloat16)
    edit_keys = jnp.dot(select, key_table, preferred_element_type=jnp.float32).astype(jnp.bfloat16)
    coeff_part = lax.dot_general(
        edit_keys, hidden_act, (((1,), (1,)), ((), ())), preferred_element_type=jnp.float32
    )
    coeff = lax.psum(coeff_part, "vocab")
    base_rows, local_values = (
        lax.all_gather(base_out, "vocab", axis=1, tiled=True),
        lax.all_gather(value_vecs, "vocab", axis=1, tiled=True),
    )
    values = lax.all_gather(local_values, "edit", axis=0, tiled=True)
    base32 = base_rows.astype(jnp.float32)
    base_norm = (norm_gain * base32 * rms_scale(base32)).astype(jnp.bfloat16)
    base_logits = lax.dot_general(
        base_norm, head, (((1,), (1,)), ((), ())), preferred_element_type=jnp.float32
    )
    edited = base32[None, :, :] + coeff[:, :, None] * values.astype(jnp.float32)[:, None, :]
    row_scale = rms_scale(edited)
    normed = (norm_gain * edited * row_scale).astype(jnp.bfloat16)
    logits = jnp.einsum("etd,vd->etv", normed, head, preferred_element_type=jnp.float32)
    vocab_start = lax.axis_index(("vocab", "edit")) * vocab_rows
    vocab_ids = vocab_start + jnp.arange(vocab_rows, dtype=jnp.int32)
    onehot = (token_ids[:, None] == vocab_ids[None, :]).astype(jnp.float32)
    peak_base = jnp.max(base_logits, axis=-1)
    peak_edit = jnp.max(logits, axis=-1)
    peak_base, peak_edit = lax.pmax((peak_base, peak_edit), ("vocab", "edit"))
    base_exp = jnp.exp(base_logits - peak_base[:, None])
    base_total = jnp.sum(base_exp, axis=-1)
    edit_total = jnp.sum(jnp.exp(logits - peak_edit[:, :, None]), axis=-1)
    cross_sum = jnp.sum(base_exp[None, :, :] * (base_logits[None, :, :] - logits), axis=-1)
    target = jnp.sum(onehot[None, :, :] * logits, axis=-1)
    base_total, edit_total, cross_sum, target = lax.psum(
        (base_total, edit_total, cross_sum, target), ("vocab", "edit")
    )
    base_lse = peak_base + jnp.log(base_total)
    edit_lse = peak_edit + jnp.log(edit_total)
    valid = valid_mask.astype(jnp.float32)
    token_kl = valid[None, :] * (cross_sum / base_total[None, :] - base_lse[None, :] + edit_lse)
    target_logprob = target - edit_lse
    base_prob = jnp.exp(base_logits - base_lse[:, None])
    edit_prob = jnp.exp(logits - edit_lse[:, :, None])
    logit_grad = (valid[None, :, None] * (edit_prob - base_prob[None, :, :])).astype(jnp.bfloat16)
    back_rows = jnp.einsum("etv,vd->etd", logit_grad, head, preferred_element_type=jnp.float32)
    grad_y = norm_gain * back_rows
    grad_o = row_scale * grad_y - edited * row_scale**3 * jnp.mean(
        grad_y * edited, axis=-1, keepdims=True
    )
    grad_part = jnp.sum(coeff[:, :, None] * grad_o, axis=1)
    edit_start = lax.axis_index("edit") * edit_rows
    grad_total = lax.psum(grad_part, ("vocab", "edit", "tok"))
    grad_mine = lax.dynamic_slice_in_dim(grad_total, edit_start, edit_rows, 0)
    grad_piece = lax.dynamic_slice_in_dim(
        grad_mine, lax.axis_index("vocab") * piece_width, piece_width, 1
    )
    kl_mine = lax.dynamic_slice_in_dim(token_kl, edit_start, edit_rows, 0)
    target_mine = lax.dynamic_slice_in_dim(target_logprob, edit_start, edit_rows, 0)
    return (grad_piece, kl_mine, target_mine)


MESH = pl.DeviceIdType.MESH


def split_rows(row, where_mask):
    hi = row.astype(jnp.bfloat16).astype(jnp.float32)
    rest = row - hi
    mid = rest.astype(jnp.bfloat16).astype(jnp.float32)
    low = rest - mid
    at = lax.broadcasted_iota(jnp.int32, (8, row.shape[1]), 0)
    rows = jnp.where(at == 0, hi, jnp.where(at == 1, mid, jnp.where(at == 2, low, 0.0)))
    return rows if where_mask is None else jnp.where(where_mask, rows, 0.0)


def fused(
    nv,
    key_hbm,
    ids_hbm,
    mask_hbm,
    act_hbm,
    table_hbm,
    base_hbm,
    val_hbm,
    gain_hbm,
    head_hbm,
    grad_ref,
    kl_ref,
    tl_ref,
    key_ref,
    ids_ref,
    mask_ref,
    table_ref,
    val_ref,
    gain_ref,
    act,
    head,
    rows_all,
    vals,
    myval,
    cpart,
    call,
    sqpart,
    sqall,
    acc,
    normed,
    stat,
    stats,
    wmine,
    wother,
    smine,
    sother,
    gpart,
    gall,
    local_sem,
    zs,
    zr,
    xs,
    xr,
    vs,
    vr,
    cs,
    cr,
    qs,
    qr,
    ss,
    sr,
    gs,
    gr,
    ts,
    tr,
):
    f32, bf16 = jnp.float32, jnp.bfloat16
    z = lax.axis_index("vocab")
    x = lax.axis_index("edit")
    c = lax.axis_index("tok")
    q = z * 2 + x
    nq = nv * 2
    tk, width = base_hbm.shape
    half = tk // 2
    dim = gain_hbm.shape[1]
    vrows = head_hbm.shape[0]
    hv = vrows // 4

    barrier = pltpu.get_barrier_semaphore()
    peers = []
    for k in range(1, nq):
        p = lax.rem(q + k, nq)
        peers.append({"vocab": p // 2, "edit": lax.rem(p, 2)})
    buddy = {"tok": 1 - c}
    for p in peers:
        pl.semaphore_signal(barrier, inc=1, device_id=p, device_id_type=MESH)
    pl.semaphore_signal(barrier, inc=1, device_id=buddy, device_id_type=MESH)

    def fetch(src, dst, i):
        d = pltpu.make_async_copy(src, dst, local_sem.at[i])
        d.start()
        return d

    val_in = fetch(val_hbm, val_ref, 0)
    base_in = fetch(base_hbm, rows_all.at[z], 1)
    small_in = [
        fetch(key_hbm, key_ref, 2),
        fetch(table_hbm, table_ref, 3),
        fetch(act_hbm, act, 4),
        fetch(ids_hbm, ids_ref, 5),
        fetch(mask_hbm, mask_ref, 6),
        fetch(gain_hbm, gain_ref, 7),
    ]
    head_in = [
        fetch(head_hbm.at[pl.ds(i * hv, hv)], head.at[pl.ds(i * hv, hv)], 8 + i) for i in range(4)
    ]
    val_in.wait()
    myval[...] = val_ref[...].astype(f32)
    vals[x, z] = myval[...]
    base_in.wait()
    pl.semaphore_wait(barrier, nq)

    mine = pl.ds(pl.multiple_of(x * half, half), half)

    def send(src, dst, ssem, rsem, dev):
        d = pltpu.make_async_remote_copy(
            src_ref=src, dst_ref=dst, send_sem=ssem, recv_sem=rsem, device_id=dev, device_id_type=MESH
        )
        d.start()
        return d

    vcopies = [
        send(myval, vals.at[x, z], vs.at[k], vr.at[k], peers[k]) for k in range(nq - 1)
    ]
    order = [1, nv - 1] + [k for k in range(2, nv - 1)]
    zcopies = {}
    for k in order:
        zcopies[k] = send(
            rows_all.at[z, mine], rows_all.at[z, mine], zs.at[k], zr.at[k], {"vocab": lax.rem(z + k, nv)}
        )

    for d in small_in:
        d.wait()
    every = lax.dot_general(
        table_ref[...], act[...], (((1,), (1,)), ((), ())), preferred_element_type=f32
    )
    slots = lax.broadcasted_iota(jnp.int32, every.shape, 0)
    for e in range(2):
        cpart[e] = jnp.sum(
            jnp.where(slots == key_ref[:, e : e + 1], every, 0.0), axis=0, keepdims=True
        )
    call[z] = cpart[...]
    ccopies = [
        send(cpart, call.at[z], cs.at[k], cr.at[k], {"vocab": lax.rem(z + k, nv)})
        for k in range(1, nv)
    ]

    sub = lax.broadcasted_iota(jnp.int32, (tk, 2 * tk), 0)
    lane = lax.broadcasted_iota(jnp.int32, (tk, 2 * tk), 1)
    first = lane < tk
    diag = jnp.where(first, lane, lane - tk) == sub
    eye = lax.broadcasted_iota(jnp.int32, (tk, tk), 0) == lax.broadcasted_iota(
        jnp.int32, (tk, tk), 1
    )

    def to_col(row):
        return jnp.sum(jnp.where(eye, row, 0.0), axis=1, keepdims=True)

    def to_row(col0, col1):
        return jnp.sum(
            jnp.where(diag, jnp.where(first, col0, col1), 0.0), axis=0, keepdims=True
        )

    ids_col = to_col(ids_ref[...].astype(f32))
    ids_row = to_row(ids_col, ids_col)
    valid_col = to_col(mask_ref[...].astype(f32))
    valid = to_row(valid_col, valid_col)

    for d in ccopies:
        d.wait_recv()
    for d in vcopies:
        d.wait_recv()
    coeff = []
    for e in range(2):
        total = call[0, e]
        for s in range(1, nv):
            total = total + call[s, e]
        coeff.append(to_col(total))
    b = rows_all[z].astype(f32)
    sq = [jnp.sum(b * b, axis=1, keepdims=True)]
    for e in range(2):
        ed = b + coeff[e] * vals[e, z]
        sq.append(jnp.sum(ed * ed, axis=1, keepdims=True))
    sqpart[0] = to_row(sq[0], sq[0])
    sqpart[1] = to_row(sq[1], sq[2])
    sqall[z] = sqpart[...]
    qcopies = [
        send(sqpart, sqall.at[z], qs.at[k], qr.at[k], {"vocab": lax.rem(z + k, nv)})
        for k in range(1, nv)
    ]
    xcopies = {}
    for k in order:
        zcopies[k].wait_recv()
        s = lax.rem(z - k + nv, nv)
        xcopies[k] = send(
            rows_all.at[s, mine], rows_all.at[s, mine], xs.at[k], xr.at[k], {"edit": 1 - x}
        )
    for d in qcopies:
        d.wait_recv()
    sqb, sqe = sqall[0, 0], sqall[0, 1]
    for s in range(1, nv):
        sqb = sqb + sqall[s, 0]
        sqe = sqe + sqall[s, 1]
    rb_row = lax.rsqrt(sqb / dim + NORM_EPS)
    re_row = lax.rsqrt(sqe / dim + NORM_EPS)
    c_row = to_row(coeff[0], coeff[1])
    in0 = lane == sub
    in1 = lane == sub + tk

    def col_of(where, row):
        return jnp.sum(jnp.where(where, row, 0.0), axis=1, keepdims=True)

    scale = [col_of(in0, rb_row), col_of(in0, re_row), col_of(in1, re_row)]
    for step, k in enumerate([0] + order):
        if step == 0:
            for d in head_in:
                d.wait()
        else:
            xcopies[k].wait_recv()
        s = lax.rem(z - k + nv, nv)
        cols = pl.ds(pl.multiple_of(s * width, width), width)
        b = rows_all[s].astype(f32)
        gain = gain_ref[:, cols]
        plain = (gain * b * scale[0]).astype(bf16)
        normed[step, 0:tk] = plain
        normed[step, tk : 2 * tk] = plain
        for e in range(2):
            ed = b + coeff[e] * vals[e, s]
            normed[step, (2 + e) * tk : (3 + e) * tk] = (gain * ed * scale[1 + e]).astype(bf16)
        part = lax.dot_general(
            head[:, cols], normed[step], (((1,), (1,)), ((), ())), preferred_element_type=f32
        )
        if step == 0:
            acc[...] = part
        else:
            acc[...] += part
    logit = acc[...]
    lb, le = logit[:, : 2 * tk], logit[:, 2 * tk :]
    vid = (q * vrows + lax.broadcasted_iota(jnp.int32, lb.shape, 0)).astype(f32)
    mb = jnp.max(lb, axis=0, keepdims=True)
    me = jnp.max(le, axis=0, keepdims=True)
    eb = jnp.exp(lb - mb)
    ee = jnp.exp(le - me)
    stat[0:1] = mb
    stat[1:2] = me
    stat[2:3] = jnp.sum(eb, axis=0, keepdims=True)
    stat[3:4] = jnp.sum(ee, axis=0, keepdims=True)
    stat[4:5] = jnp.sum(eb * (lb - le), axis=0, keepdims=True)
    stat[5:6] = jnp.sum(eb * le, axis=0, keepdims=True)
    stat[6:7] = jnp.sum(ee * le, axis=0, keepdims=True)
    stat[7:8] = jnp.sum(jnp.where(vid == ids_row, le, 0.0), axis=0, keepdims=True)
    stats[q] = stat[...]
    scopies = [send(stat, stats.at[q], ss.at[k], sr.at[k], peers[k]) for k in range(nq - 1)]
    cr_row = c_row * re_row
    crr_row = cr_row * re_row
    lanes8 = lax.broadcasted_iota(jnp.int32, (8, 2 * tk), 1)
    lhs = jnp.concatenate(
        [split_rows(cr_row, lanes8 < tk), split_rows(cr_row, lanes8 >= tk)], axis=0
    ).astype(bf16)
    for d in scopies:
        d.wait_recv()

    pb, pe = stats[0, 0:1], stats[0, 1:2]
    for p in range(1, nq):
        pb = jnp.maximum(pb, stats[p, 0:1])
        pe = jnp.maximum(pe, stats[p, 1:2])
    sums = [jnp.zeros((1, 2 * tk), f32) for _ in range(6)]
    for p in range(nq):
        fb = jnp.exp(stats[p, 0:1] - pb)
        fe = jnp.exp(stats[p, 1:2] - pe)
        for j, f in enumerate((fb, fe, fb, fb, fe, None)):
            got = stats[p, 2 + j : 3 + j]
            sums[j] = sums[j] + (got if f is None else f * got)
    tb, te, cross, meanb, meane, target = sums
    lse_b = pb + jnp.log(tb)
    lse_e = pe + jnp.log(te)
    lg = (valid * (jnp.exp(le - lse_e) - jnp.exp(lb - lse_b))).astype(bf16)
    w = lax.dot_general(lhs, lg, (((1,), (1,)), ((), ())), preferred_element_type=f32)
    wmine[0] = jnp.sum(w[0:8], axis=0, keepdims=True)
    wmine[1] = jnp.sum(w[8:16], axis=0, keepdims=True)
    wcopy = send(wmine, wother, ts.at[0], tr.at[0], buddy)

    pull = crr_row * valid * (meane / te - meanb / tb) / dim
    own = lane - tk * x == sub
    pull_col = jnp.sum(jnp.where(own, pull, 0.0), axis=1, keepdims=True)
    own_coeff = jnp.where(x == 0, coeff[0], coeff[1])
    ed = rows_all[z].astype(f32) + own_coeff * myval[...]
    smine[...] = jnp.sum(pull_col * ed, axis=0, keepdims=True)
    scopy = send(smine, sother, ts.at[1], tr.at[1], buddy)
    kl = valid * (cross / tb - lse_b + lse_e)
    tl = target - lse_e
    kl_ref[...] = jnp.where(x == 0, kl, pltpu.roll(kl, tk, 1))[:, :tk]
    tl_ref[...] = jnp.where(x == 0, tl, pltpu.roll(tl, tk, 1))[:, :tk]

    wcopy.wait_recv()
    wl = jnp.concatenate(
        [split_rows(wmine[e] + wother[e], None) for e in range(2)], axis=0
    ).astype(bf16)
    back = lax.dot_general(wl, head[...], (((1,), (0,)), ((), ())), preferred_element_type=f32)
    for e in range(2):
        g = jnp.sum(back[e * 8 : e * 8 + 8], axis=0, keepdims=True) * gain_ref[...]
        for s in range(nv):
            gpart[e, s] = g[:, s * width : (s + 1) * width]
    gall[q] = gpart[x, z]
    gcopies = []
    for k in range(nq - 1):
        p = peers[k]
        gcopies.append(send(gpart.at[p["edit"], p["vocab"]], gall.at[q], gs.at[k], gr.at[k], p))
    scopy.wait_recv()
    out = -(smine[...] + sother[...])
    for d in gcopies:
        d.wait_recv()
    for p in range(nq):
        out = out + gall[p]
    grad_ref[...] = out
    for d in list(zcopies.values()) + list(xcopies.values()) + vcopies + ccopies + qcopies + scopies + gcopies:
        d.wait_send()
    wcopy.wait_send()
    scopy.wait_send()


def kernel_device(
    nv, token_ids, valid_mask, key_index, hidden_act, key_table, base_out, value_vecs, norm_gain, head
):
    f32, bf16 = jnp.float32, jnp.bfloat16
    tk, width = base_out.shape
    dim = head.shape[1]
    vrows = head.shape[0]
    nq = nv * 2
    dma = lambda n: pltpu.SemaphoreType.DMA((n,))
    vmem = pl.BlockSpec(memory_space=pltpu.VMEM)
    hbm = pl.BlockSpec(memory_space=pltpu.HBM)
    return pl.pallas_call(
        functools.partial(fused, nv),
        out_shape=(
            jax.ShapeDtypeStruct((1, width), f32),
            jax.ShapeDtypeStruct((1, tk), f32),
            jax.ShapeDtypeStruct((1, tk), f32),
        ),
        in_specs=[hbm] * 9,
        out_specs=(vmem, vmem, vmem),
        scratch_shapes=[
            pltpu.VMEM((1, 2), jnp.int32),
            pltpu.VMEM((1, tk), jnp.int32),
            pltpu.VMEM((1, tk), jnp.int32),
            pltpu.VMEM(key_table.shape, bf16),
            pltpu.VMEM((1, width), bf16),
            pltpu.VMEM((1, dim), f32),
            pltpu.VMEM(hidden_act.shape, bf16),
            pltpu.VMEM(head.shape, bf16),
            pltpu.VMEM((nv, tk, width), bf16),
            pltpu.VMEM((2, nv, 1, width), f32),
            pltpu.VMEM((1, width), f32),
            pltpu.VMEM((2, 1, tk), f32),
            pltpu.VMEM((nv, 2, 1, tk), f32),
            pltpu.VMEM((2, 1, 2 * tk), f32),
            pltpu.VMEM((nv, 2, 1, 2 * tk), f32),
            pltpu.VMEM((vrows, 4 * tk), f32),
            pltpu.VMEM((nv, 4 * tk, width), bf16),
            pltpu.VMEM((8, 2 * tk), f32),
            pltpu.VMEM((nq, 8, 2 * tk), f32),
            pltpu.VMEM((2, 1, vrows), f32),
            pltpu.VMEM((2, 1, vrows), f32),
            pltpu.VMEM((1, width), f32),
            pltpu.VMEM((1, width), f32),
            pltpu.VMEM((2, nv, 1, width), f32),
            pltpu.VMEM((nq, 1, width), f32),
            dma(12),
            dma(nv), dma(nv), dma(nv), dma(nv),
            dma(nq), dma(nq), dma(nv), dma(nv), dma(nv), dma(nv),
            dma(nq), dma(nq), dma(nq), dma(nq),
            dma(2), dma(2),
        ],
        compiler_params=pltpu.CompilerParams(
            collective_id=0, has_side_effects=True, vmem_limit_bytes=64 * 1024 * 1024
        ),
    )(
        key_index.reshape(1, 2),
        token_ids.reshape(1, tk),
        valid_mask.reshape(1, tk),
        hidden_act,
        key_table,
        base_out,
        value_vecs,
        norm_gain.reshape(1, dim),
        head,
    )


def solution(mesh):
    placed = (
        P(("groups", "tok")),
        P(("groups", "tok")),
        P("groups"),
        P(("groups", "tok"), "vocab"),
        P(None, "vocab"),
        P(("groups", "tok"), "vocab"),
        P(("groups", "edit"), "vocab"),
        P(),
        P(("vocab", "edit"), None),
    )
    body = per_device
    if mesh.shape["edit"] == 2 and mesh.shape["tok"] == 2 and 3 <= mesh.shape["vocab"] <= 4:
        body = functools.partial(kernel_device, mesh.shape["vocab"])
    return jax.shard_map(
        body,
        mesh=mesh,
        in_specs=placed,
        out_specs=(
            P(("groups", "edit"), "vocab"),
            P(("groups", "edit"), "tok"),
            P(("groups", "edit"), "tok"),
        ),
        check_vma=False,
    )
```

```python
import functools

import jax
import jax.numpy as jnp
from jax import lax
from jax.experimental import pallas as pl
from jax.experimental.pallas import tpu as pltpu
from jax.sharding import PartitionSpec as P

NORM_EPS = 1e-05


def rms_scale(hidden_rows):
    return lax.rsqrt(jnp.mean(hidden_rows * hidden_rows, axis=-1, keepdims=True) + NORM_EPS)


def per_device(
    token_ids, valid_mask, key_index, hidden_act, key_table, base_out, value_vecs, norm_gain, head
):
    vocab_rows = head.shape[0]
    edit_rows = value_vecs.shape[0]
    piece_width = value_vecs.shape[1]
    key_slots = jnp.arange(key_table.shape[0], dtype=jnp.int32)
    select = (key_index[:, None] == key_slots[None, :]).astype(jnp.bfloat16)
    edit_keys = jnp.dot(select, key_table, preferred_element_type=jnp.float32).astype(jnp.bfloat16)
    coeff_part = lax.dot_general(
        edit_keys, hidden_act, (((1,), (1,)), ((), ())), preferred_element_type=jnp.float32
    )
    coeff = lax.psum(coeff_part, "vocab")
    base_rows, local_values = (
        lax.all_gather(base_out, "vocab", axis=1, tiled=True),
        lax.all_gather(value_vecs, "vocab", axis=1, tiled=True),
    )
    values = lax.all_gather(local_values, "edit", axis=0, tiled=True)
    base32 = base_rows.astype(jnp.float32)
    base_norm = (norm_gain * base32 * rms_scale(base32)).astype(jnp.bfloat16)
    base_logits = lax.dot_general(
        base_norm, head, (((1,), (1,)), ((), ())), preferred_element_type=jnp.float32
    )
    edited = base32[None, :, :] + coeff[:, :, None] * values.astype(jnp.float32)[:, None, :]
    row_scale = rms_scale(edited)
    normed = (norm_gain * edited * row_scale).astype(jnp.bfloat16)
    logits = jnp.einsum("etd,vd->etv", normed, head, preferred_element_type=jnp.float32)
    vocab_start = lax.axis_index(("vocab", "edit")) * vocab_rows
    vocab_ids = vocab_start + jnp.arange(vocab_rows, dtype=jnp.int32)
    onehot = (token_ids[:, None] == vocab_ids[None, :]).astype(jnp.float32)
    peak_base = jnp.max(base_logits, axis=-1)
    peak_edit = jnp.max(logits, axis=-1)
    peak_base, peak_edit = lax.pmax((peak_base, peak_edit), ("vocab", "edit"))
    base_exp = jnp.exp(base_logits - peak_base[:, None])
    base_total = jnp.sum(base_exp, axis=-1)
    edit_total = jnp.sum(jnp.exp(logits - peak_edit[:, :, None]), axis=-1)
    cross_sum = jnp.sum(base_exp[None, :, :] * (base_logits[None, :, :] - logits), axis=-1)
    target = jnp.sum(onehot[None, :, :] * logits, axis=-1)
    base_total, edit_total, cross_sum, target = lax.psum(
        (base_total, edit_total, cross_sum, target), ("vocab", "edit")
    )
    base_lse = peak_base + jnp.log(base_total)
    edit_lse = peak_edit + jnp.log(edit_total)
    valid = valid_mask.astype(jnp.float32)
    token_kl = valid[None, :] * (cross_sum / base_total[None, :] - base_lse[None, :] + edit_lse)
    target_logprob = target - edit_lse
    base_prob = jnp.exp(base_logits - base_lse[:, None])
    edit_prob = jnp.exp(logits - edit_lse[:, :, None])
    logit_grad = (valid[None, :, None] * (edit_prob - base_prob[None, :, :])).astype(jnp.bfloat16)
    back_rows = jnp.einsum("etv,vd->etd", logit_grad, head, preferred_element_type=jnp.float32)
    grad_y = norm_gain * back_rows
    grad_o = row_scale * grad_y - edited * row_scale**3 * jnp.mean(
        grad_y * edited, axis=-1, keepdims=True
    )
    grad_part = jnp.sum(coeff[:, :, None] * grad_o, axis=1)
    edit_start = lax.axis_index("edit") * edit_rows
    grad_total = lax.psum(grad_part, ("vocab", "edit", "tok"))
    grad_mine = lax.dynamic_slice_in_dim(grad_total, edit_start, edit_rows, 0)
    grad_piece = lax.dynamic_slice_in_dim(
        grad_mine, lax.axis_index("vocab") * piece_width, piece_width, 1
    )
    kl_mine = lax.dynamic_slice_in_dim(token_kl, edit_start, edit_rows, 0)
    target_mine = lax.dynamic_slice_in_dim(target_logprob, edit_start, edit_rows, 0)
    return (grad_piece, kl_mine, target_mine)


MESH = pl.DeviceIdType.MESH


def split_rows(row, where_mask):
    hi = row.astype(jnp.bfloat16).astype(jnp.float32)
    rest = row - hi
    mid = rest.astype(jnp.bfloat16).astype(jnp.float32)
    low = rest - mid
    at = lax.broadcasted_iota(jnp.int32, (8, row.shape[1]), 0)
    rows = jnp.where(at == 0, hi, jnp.where(at == 1, mid, jnp.where(at == 2, low, 0.0)))
    return rows if where_mask is None else jnp.where(where_mask, rows, 0.0)


def fused(
    nv,
    key_hbm,
    ids_hbm,
    mask_hbm,
    act_hbm,
    table_hbm,
    base_hbm,
    val_hbm,
    gain_hbm,
    head_hbm,
    grad_ref,
    kl_ref,
    tl_ref,
    key_ref,
    ids_ref,
    mask_ref,
    table_ref,
    val_ref,
    gain_ref,
    act,
    head,
    rows_all,
    vals,
    myval,
    cpart,
    call,
    sqpart,
    sqall,
    acc,
    normed,
    stat,
    stats,
    wmine,
    wother,
    smine,
    sother,
    gpart,
    gall,
    local_sem,
    zs,
    zf,
    zr,
    xs,
    xr,
    vs,
    vr,
    cs,
    cr,
    qs,
    qr,
    ss,
    sr,
    gs,
    gr,
    ts,
    tr,
):
    f32, bf16 = jnp.float32, jnp.bfloat16
    z = lax.axis_index("vocab")
    x = lax.axis_index("edit")
    c = lax.axis_index("tok")
    q = z * 2 + x
    nq = nv * 2
    tk, width = base_hbm.shape
    half = tk // 2
    dim = gain_hbm.shape[1]
    vrows = head_hbm.shape[0]
    hv = vrows // 4

    barrier = pltpu.get_barrier_semaphore()
    peers = []
    for k in range(1, nq):
        p = lax.rem(q + k, nq)
        peers.append({"vocab": p // 2, "edit": lax.rem(p, 2)})
    buddy = {"tok": 1 - c}
    for p in peers:
        pl.semaphore_signal(barrier, inc=1, device_id=p, device_id_type=MESH)
    pl.semaphore_signal(barrier, inc=1, device_id=buddy, device_id_type=MESH)

    def fetch(src, dst, i):
        d = pltpu.make_async_copy(src, dst, local_sem.at[i])
        d.start()
        return d

    val_in = fetch(val_hbm, val_ref, 0)
    base_in = fetch(base_hbm, rows_all.at[z], 1)
    small_in = [
        fetch(key_hbm, key_ref, 2),
        fetch(table_hbm, table_ref, 3),
        fetch(act_hbm, act, 4),
        fetch(ids_hbm, ids_ref, 5),
        fetch(mask_hbm, mask_ref, 6),
        fetch(gain_hbm, gain_ref, 7),
    ]
    head_in = [
        fetch(head_hbm.at[pl.ds(i * hv, hv)], head.at[pl.ds(i * hv, hv)], 8 + i) for i in range(4)
    ]
    val_in.wait()
    myval[...] = val_ref[...].astype(f32)
    vals[x, z] = myval[...]
    base_in.wait()
    for d in small_in:
        d.wait()
    every = lax.dot_general(
        table_ref[...], act[...], (((1,), (1,)), ((), ())), preferred_element_type=f32
    )
    slots = lax.broadcasted_iota(jnp.int32, every.shape, 0)
    for e in range(2):
        cpart[e] = jnp.sum(
            jnp.where(slots == key_ref[:, e : e + 1], every, 0.0), axis=0, keepdims=True
        )
    call[z] = cpart[...]
    pl.semaphore_wait(barrier, nq)

    quarter = half // 2

    def piece(h, sub):
        return pl.ds(pl.multiple_of(h * half + sub * quarter, quarter), quarter)

    def remote(src, dst, ssem, rsem, dev):
        return pltpu.make_async_remote_copy(
            src_ref=src, dst_ref=dst, send_sem=ssem, recv_sem=rsem, device_id=dev, device_id_type=MESH
        )

    def send(src, dst, ssem, rsem, dev):
        d = remote(src, dst, ssem, rsem, dev)
        d.start()
        return d

    def along(s, sub, ssem, to):
        ref = rows_all.at[s, piece(x, sub)]
        return remote(ref, ref, ssem, zr.at[s * 2 + sub], {"vocab": to})

    def across(s, h, sub, ssem):
        ref = rows_all.at[s, piece(h, sub)]
        return remote(ref, ref, ssem, xr.at[s * 2 + sub], {"edit": 1 - x})

    first_s = z + 1 - 2 * ((z + 3) // 4)
    third_s = 3 * (1 - z // 2)
    steps = [first_s, 6 - z - first_s - third_s, third_s]
    onward = [z + 1, z - 1, 3 * z - 3]
    middle = z * (3 - z) > 0
    for sub in range(2):

        @pl.when(z < nv - 1)
        def _():
            along(z, sub, zs.at[sub], z + 1).start()

        @pl.when(z > 0)
        def _():
            along(z, sub, zs.at[2 + sub], z - 1).start()

    ccopies = [
        send(cpart, call.at[z], cs.at[k], cr.at[k], {"vocab": lax.rem(z + k, nv)})
        for k in range(1, nv)
    ]

    vcopies = [
        send(myval, vals.at[x, z], vs.at[k], vr.at[k], peers[k]) for k in range(nq - 1)
    ]

    def pass_on(i):
        for sub in range(2):
            at = i * 2 + sub
            along(steps[i], sub, zf.at[at], z).wait_recv()

            @pl.when(middle)
            def _():
                along(steps[i], sub, zf.at[at], onward[i]).start()

            across(steps[i], x, sub, xs.at[at]).start()

    row_at = lax.broadcasted_iota(jnp.int32, (tk, 2 * tk), 0)
    lane = lax.broadcasted_iota(jnp.int32, (tk, 2 * tk), 1)
    first = lane < tk
    diag = jnp.where(first, lane, lane - tk) == row_at
    eye = lax.broadcasted_iota(jnp.int32, (tk, tk), 0) == lax.broadcasted_iota(
        jnp.int32, (tk, tk), 1
    )

    def to_col(row):
        return jnp.sum(jnp.where(eye, row, 0.0), axis=1, keepdims=True)

    def to_row(col0, col1):
        return jnp.sum(
            jnp.where(diag, jnp.where(first, col0, col1), 0.0), axis=0, keepdims=True
        )

    ids_col = to_col(ids_ref[...].astype(f32))
    ids_row = to_row(ids_col, ids_col)
    valid_col = to_col(mask_ref[...].astype(f32))
    valid = to_row(valid_col, valid_col)

    pass_on(0)
    for d in ccopies:
        d.wait_recv()
    for d in vcopies:
        d.wait_recv()
    coeff = []
    for e in range(2):
        total = call[0, e]
        for s in range(1, nv):
            total = total + call[s, e]
        coeff.append(to_col(total))
    b = rows_all[z].astype(f32)
    sq = [jnp.sum(b * b, axis=1, keepdims=True)]
    for e in range(2):
        ed = b + coeff[e] * vals[e, z]
        sq.append(jnp.sum(ed * ed, axis=1, keepdims=True))
    sqpart[0] = to_row(sq[0], sq[0])
    sqpart[1] = to_row(sq[1], sq[2])
    sqall[z] = sqpart[...]
    qcopies = [
        send(sqpart, sqall.at[z], qs.at[k], qr.at[k], {"vocab": lax.rem(z + k, nv)})
        for k in range(1, nv)
    ]
    pass_on(1)
    pass_on(2)
    for d in qcopies:
        d.wait_recv()
    sqb, sqe = sqall[0, 0], sqall[0, 1]
    for s in range(1, nv):
        sqb = sqb + sqall[s, 0]
        sqe = sqe + sqall[s, 1]
    rb_row = lax.rsqrt(sqb / dim + NORM_EPS)
    re_row = lax.rsqrt(sqe / dim + NORM_EPS)
    c_row = to_row(coeff[0], coeff[1])
    in0 = lane == row_at
    in1 = lane == row_at + tk

    def col_of(where, row):
        return jnp.sum(jnp.where(where, row, 0.0), axis=1, keepdims=True)

    scale = [col_of(in0, rb_row), col_of(in0, re_row), col_of(in1, re_row)]
    for step in range(nv):
        if step == 0:
            for d in head_in:
                d.wait()
        else:
            for sub in range(2):
                across(steps[step - 1], 1 - x, sub, xs.at[0]).wait_recv()
        s = z if step == 0 else steps[step - 1]
        cols = pl.ds(pl.multiple_of(s * width, width), width)
        b = rows_all[s].astype(f32)
        gain = gain_ref[:, cols]
        plain = (gain * b * scale[0]).astype(bf16)
        normed[step, 0:tk] = plain
        normed[step, tk : 2 * tk] = plain
        for e in range(2):
            ed = b + coeff[e] * vals[e, s]
            normed[step, (2 + e) * tk : (3 + e) * tk] = (gain * ed * scale[1 + e]).astype(bf16)
        part = lax.dot_general(
            head[:, cols], normed[step], (((1,), (1,)), ((), ())), preferred_element_type=f32
        )
        if step == 0:
            acc[...] = part
        else:
            acc[...] += part
    logit = acc[...]
    lb, le = logit[:, : 2 * tk], logit[:, 2 * tk :]
    vid = (q * vrows + lax.broadcasted_iota(jnp.int32, lb.shape, 0)).astype(f32)
    mb = jnp.max(lb, axis=0, keepdims=True)
    me = jnp.max(le, axis=0, keepdims=True)
    eb = jnp.exp(lb - mb)
    ee = jnp.exp(le - me)
    stat[0:1] = mb
    stat[1:2] = me
    stat[2:3] = jnp.sum(eb, axis=0, keepdims=True)
    stat[3:4] = jnp.sum(ee, axis=0, keepdims=True)
    stat[4:5] = jnp.sum(eb * (lb - le), axis=0, keepdims=True)
    stat[5:6] = jnp.sum(eb * le, axis=0, keepdims=True)
    stat[6:7] = jnp.sum(ee * le, axis=0, keepdims=True)
    stat[7:8] = jnp.sum(jnp.where(vid == ids_row, le, 0.0), axis=0, keepdims=True)
    stats[q] = stat[...]
    scopies = [send(stat, stats.at[q], ss.at[k], sr.at[k], peers[k]) for k in range(nq - 1)]
    cr_row = c_row * re_row
    crr_row = cr_row * re_row
    lanes8 = lax.broadcasted_iota(jnp.int32, (8, 2 * tk), 1)
    lhs = jnp.concatenate(
        [split_rows(cr_row, lanes8 < tk), split_rows(cr_row, lanes8 >= tk)], axis=0
    ).astype(bf16)
    for d in scopies:
        d.wait_recv()

    pb, pe = stats[0, 0:1], stats[0, 1:2]
    for p in range(1, nq):
        pb = jnp.maximum(pb, stats[p, 0:1])
        pe = jnp.maximum(pe, stats[p, 1:2])
    sums = [jnp.zeros((1, 2 * tk), f32) for _ in range(6)]
    for p in range(nq):
        fb = jnp.exp(stats[p, 0:1] - pb)
        fe = jnp.exp(stats[p, 1:2] - pe)
        for j, f in enumerate((fb, fe, fb, fb, fe, None)):
            got = stats[p, 2 + j : 3 + j]
            sums[j] = sums[j] + (got if f is None else f * got)
    tb, te, cross, meanb, meane, target = sums
    lse_b = pb + jnp.log(tb)
    lse_e = pe + jnp.log(te)
    lg = (valid * (jnp.exp(le - lse_e) - jnp.exp(lb - lse_b))).astype(bf16)
    w = lax.dot_general(lhs, lg, (((1,), (1,)), ((), ())), preferred_element_type=f32)
    wmine[0] = jnp.sum(w[0:8], axis=0, keepdims=True)
    wmine[1] = jnp.sum(w[8:16], axis=0, keepdims=True)
    wcopy = send(wmine, wother, ts.at[0], tr.at[0], buddy)

    pull = crr_row * valid * (meane / te - meanb / tb) / dim
    own = lane - tk * x == row_at
    pull_col = jnp.sum(jnp.where(own, pull, 0.0), axis=1, keepdims=True)
    own_coeff = jnp.where(x == 0, coeff[0], coeff[1])
    ed = rows_all[z].astype(f32) + own_coeff * myval[...]
    smine[...] = jnp.sum(pull_col * ed, axis=0, keepdims=True)
    scopy = send(smine, sother, ts.at[1], tr.at[1], buddy)
    kl = valid * (cross / tb - lse_b + lse_e)
    tl = target - lse_e
    kl_ref[...] = jnp.where(x == 0, kl, pltpu.roll(kl, tk, 1))[:, :tk]
    tl_ref[...] = jnp.where(x == 0, tl, pltpu.roll(tl, tk, 1))[:, :tk]

    wcopy.wait_recv()
    wl = jnp.concatenate(
        [split_rows(wmine[e] + wother[e], None) for e in range(2)], axis=0
    ).astype(bf16)
    back = lax.dot_general(wl, head[...], (((1,), (0,)), ((), ())), preferred_element_type=f32)
    for e in range(2):
        g = jnp.sum(back[e * 8 : e * 8 + 8], axis=0, keepdims=True) * gain_ref[...]
        for s in range(nv):
            gpart[e, s] = g[:, s * width : (s + 1) * width]
    gall[q] = gpart[x, z]
    gcopies = []
    for k in range(nq - 1):
        p = peers[k]
        gcopies.append(send(gpart.at[p["edit"], p["vocab"]], gall.at[q], gs.at[k], gr.at[k], p))
    scopy.wait_recv()
    out = -(smine[...] + sother[...])
    for d in gcopies:
        d.wait_recv()
    for p in range(nq):
        out = out + gall[p]
    grad_ref[...] = out
    for sub in range(2):

        @pl.when(z < nv - 1)
        def _():
            along(z, sub, zs.at[sub], z + 1).wait_send()

        @pl.when(z > 0)
        def _():
            along(z, sub, zs.at[2 + sub], z - 1).wait_send()

        for i in range(3):

            @pl.when(middle)
            def _():
                along(steps[i], sub, zf.at[i * 2 + sub], onward[i]).wait_send()

            across(steps[i], x, sub, xs.at[i * 2 + sub]).wait_send()

    for d in vcopies + ccopies + qcopies + scopies + gcopies:
        d.wait_send()
    wcopy.wait_send()
    scopy.wait_send()


def hand_out(a_ref, b_ref, c_ref, a_out, b_out, c_out, sem):
    moves = [
        pltpu.make_async_copy(src, dst, sem.at[i])
        for i, (src, dst) in enumerate(((a_ref, a_out), (b_ref, b_out), (c_ref, c_out)))
    ]
    for d in moves:
        d.start()
    for d in moves:
        d.wait()


def kernel_device(
    nv, token_ids, valid_mask, key_index, hidden_act, key_table, base_out, value_vecs, norm_gain, head
):
    f32, bf16 = jnp.float32, jnp.bfloat16
    tk, width = base_out.shape
    dim = head.shape[1]
    vrows = head.shape[0]
    nq = nv * 2
    dma = lambda n: pltpu.SemaphoreType.DMA((n,))
    vmem = pl.BlockSpec(memory_space=pltpu.VMEM)
    hbm = pl.BlockSpec(memory_space=pltpu.HBM)
    shapes = (
        jax.ShapeDtypeStruct((1, width), f32),
        jax.ShapeDtypeStruct((1, tk), f32),
        jax.ShapeDtypeStruct((1, tk), f32),
    )
    parts = pl.pallas_call(
        functools.partial(fused, nv),
        out_shape=shapes,
        in_specs=[hbm] * 9,
        out_specs=(vmem, vmem, vmem),
        scratch_shapes=[
            pltpu.VMEM((1, 2), jnp.int32),
            pltpu.VMEM((1, tk), jnp.int32),
            pltpu.VMEM((1, tk), jnp.int32),
            pltpu.VMEM(key_table.shape, bf16),
            pltpu.VMEM((1, width), bf16),
            pltpu.VMEM((1, dim), f32),
            pltpu.VMEM(hidden_act.shape, bf16),
            pltpu.VMEM(head.shape, bf16),
            pltpu.VMEM((nv, tk, width), bf16),
            pltpu.VMEM((2, nv, 1, width), f32),
            pltpu.VMEM((1, width), f32),
            pltpu.VMEM((2, 1, tk), f32),
            pltpu.VMEM((nv, 2, 1, tk), f32),
            pltpu.VMEM((2, 1, 2 * tk), f32),
            pltpu.VMEM((nv, 2, 1, 2 * tk), f32),
            pltpu.VMEM((vrows, 4 * tk), f32),
            pltpu.VMEM((nv, 4 * tk, width), bf16),
            pltpu.VMEM((8, 2 * tk), f32),
            pltpu.VMEM((nq, 8, 2 * tk), f32),
            pltpu.VMEM((2, 1, vrows), f32),
            pltpu.VMEM((2, 1, vrows), f32),
            pltpu.VMEM((1, width), f32),
            pltpu.VMEM((1, width), f32),
            pltpu.VMEM((2, nv, 1, width), f32),
            pltpu.VMEM((nq, 1, width), f32),
            dma(12),
            dma(4), dma(6), dma(2 * nv), dma(6), dma(2 * nv),
            dma(nq), dma(nq), dma(nv), dma(nv), dma(nv), dma(nv),
            dma(nq), dma(nq), dma(nq), dma(nq),
            dma(2), dma(2),
        ],
        compiler_params=pltpu.CompilerParams(
            collective_id=0, has_side_effects=True, vmem_limit_bytes=64 * 1024 * 1024
        ),
    )(
        key_index.reshape(1, 2),
        token_ids.reshape(1, tk),
        valid_mask.reshape(1, tk),
        hidden_act,
        key_table,
        base_out,
        value_vecs,
        norm_gain.reshape(1, dim),
        head,
    )
    return pl.pallas_call(
        hand_out,
        out_shape=shapes,
        in_specs=[hbm] * 3,
        out_specs=(hbm,) * 3,
        scratch_shapes=[dma(3)],
    )(*parts)


def solution(mesh):
    placed = (
        P(("groups", "tok")),
        P(("groups", "tok")),
        P("groups"),
        P(("groups", "tok"), "vocab"),
        P(None, "vocab"),
        P(("groups", "tok"), "vocab"),
        P(("groups", "edit"), "vocab"),
        P(),
        P(("vocab", "edit"), None),
    )
    body = per_device
    if mesh.shape["edit"] == 2 and mesh.shape["tok"] == 2 and mesh.shape["vocab"] == 4:
        body = functools.partial(kernel_device, mesh.shape["vocab"])
    return jax.shard_map(
        body,
        mesh=mesh,
        in_specs=placed,
        out_specs=(
            P(("groups", "edit"), "vocab"),
            P(("groups", "edit"), "tok"),
            P(("groups", "edit"), "tok"),
        ),
        check_vma=False,
    )
```

```python
import functools

import jax
import jax.numpy as jnp
from jax import lax
from jax.experimental import pallas as pl
from jax.experimental.pallas import tpu as pltpu
from jax.sharding import PartitionSpec as P

NORM_EPS = 1e-05


def rms_scale(hidden_rows):
    return lax.rsqrt(jnp.mean(hidden_rows * hidden_rows, axis=-1, keepdims=True) + NORM_EPS)


def per_device(
    token_ids, valid_mask, key_index, hidden_act, key_table, base_out, value_vecs, norm_gain, head
):
    vocab_rows = head.shape[0]
    edit_rows = value_vecs.shape[0]
    piece_width = value_vecs.shape[1]
    key_slots = jnp.arange(key_table.shape[0], dtype=jnp.int32)
    select = (key_index[:, None] == key_slots[None, :]).astype(jnp.bfloat16)
    edit_keys = jnp.dot(select, key_table, preferred_element_type=jnp.float32).astype(jnp.bfloat16)
    coeff_part = lax.dot_general(
        edit_keys, hidden_act, (((1,), (1,)), ((), ())), preferred_element_type=jnp.float32
    )
    coeff = lax.psum(coeff_part, "vocab")
    base_rows, local_values = (
        lax.all_gather(base_out, "vocab", axis=1, tiled=True),
        lax.all_gather(value_vecs, "vocab", axis=1, tiled=True),
    )
    values = lax.all_gather(local_values, "edit", axis=0, tiled=True)
    base32 = base_rows.astype(jnp.float32)
    base_norm = (norm_gain * base32 * rms_scale(base32)).astype(jnp.bfloat16)
    base_logits = lax.dot_general(
        base_norm, head, (((1,), (1,)), ((), ())), preferred_element_type=jnp.float32
    )
    edited = base32[None, :, :] + coeff[:, :, None] * values.astype(jnp.float32)[:, None, :]
    row_scale = rms_scale(edited)
    normed = (norm_gain * edited * row_scale).astype(jnp.bfloat16)
    logits = jnp.einsum("etd,vd->etv", normed, head, preferred_element_type=jnp.float32)
    vocab_start = lax.axis_index(("vocab", "edit")) * vocab_rows
    vocab_ids = vocab_start + jnp.arange(vocab_rows, dtype=jnp.int32)
    onehot = (token_ids[:, None] == vocab_ids[None, :]).astype(jnp.float32)
    peak_base = jnp.max(base_logits, axis=-1)
    peak_edit = jnp.max(logits, axis=-1)
    peak_base, peak_edit = lax.pmax((peak_base, peak_edit), ("vocab", "edit"))
    base_exp = jnp.exp(base_logits - peak_base[:, None])
    base_total = jnp.sum(base_exp, axis=-1)
    edit_total = jnp.sum(jnp.exp(logits - peak_edit[:, :, None]), axis=-1)
    cross_sum = jnp.sum(base_exp[None, :, :] * (base_logits[None, :, :] - logits), axis=-1)
    target = jnp.sum(onehot[None, :, :] * logits, axis=-1)
    base_total, edit_total, cross_sum, target = lax.psum(
        (base_total, edit_total, cross_sum, target), ("vocab", "edit")
    )
    base_lse = peak_base + jnp.log(base_total)
    edit_lse = peak_edit + jnp.log(edit_total)
    valid = valid_mask.astype(jnp.float32)
    token_kl = valid[None, :] * (cross_sum / base_total[None, :] - base_lse[None, :] + edit_lse)
    target_logprob = target - edit_lse
    base_prob = jnp.exp(base_logits - base_lse[:, None])
    edit_prob = jnp.exp(logits - edit_lse[:, :, None])
    logit_grad = (valid[None, :, None] * (edit_prob - base_prob[None, :, :])).astype(jnp.bfloat16)
    back_rows = jnp.einsum("etv,vd->etd", logit_grad, head, preferred_element_type=jnp.float32)
    grad_y = norm_gain * back_rows
    grad_o = row_scale * grad_y - edited * row_scale**3 * jnp.mean(
        grad_y * edited, axis=-1, keepdims=True
    )
    grad_part = jnp.sum(coeff[:, :, None] * grad_o, axis=1)
    edit_start = lax.axis_index("edit") * edit_rows
    grad_total = lax.psum(grad_part, ("vocab", "edit", "tok"))
    grad_mine = lax.dynamic_slice_in_dim(grad_total, edit_start, edit_rows, 0)
    grad_piece = lax.dynamic_slice_in_dim(
        grad_mine, lax.axis_index("vocab") * piece_width, piece_width, 1
    )
    kl_mine = lax.dynamic_slice_in_dim(token_kl, edit_start, edit_rows, 0)
    target_mine = lax.dynamic_slice_in_dim(target_logprob, edit_start, edit_rows, 0)
    return (grad_piece, kl_mine, target_mine)


MESH = pl.DeviceIdType.MESH


def split_rows(row, where_mask):
    hi = row.astype(jnp.bfloat16).astype(jnp.float32)
    rest = row - hi
    mid = rest.astype(jnp.bfloat16).astype(jnp.float32)
    low = rest - mid
    at = lax.broadcasted_iota(jnp.int32, (8, row.shape[1]), 0)
    rows = jnp.where(at == 0, hi, jnp.where(at == 1, mid, jnp.where(at == 2, low, 0.0)))
    return rows if where_mask is None else jnp.where(where_mask, rows, 0.0)


def fused(
    nv,
    key_hbm,
    ids_hbm,
    mask_hbm,
    act_hbm,
    table_hbm,
    base_hbm,
    val_hbm,
    gain_hbm,
    head_hbm,
    grad_ref,
    kl_ref,
    tl_ref,
    key_ref,
    ids_ref,
    mask_ref,
    table_ref,
    val_ref,
    gain_ref,
    act,
    head,
    rows_all,
    vals,
    myval,
    cpart,
    call,
    sqpart,
    sqall,
    acc,
    normed,
    stat,
    stats,
    wmine,
    wother,
    smine,
    sother,
    gpart,
    gall,
    local_sem,
    zs,
    zf,
    zr,
    xs,
    xr,
    vs,
    vr,
    cs,
    cr,
    qs,
    qr,
    ss,
    sr,
    gs,
    gr,
    ts,
    tr,
):
    f32, bf16 = jnp.float32, jnp.bfloat16
    z = lax.axis_index("vocab")
    x = lax.axis_index("edit")
    c = lax.axis_index("tok")
    q = z * 2 + x
    nq = nv * 2
    tk, width = base_hbm.shape
    half = tk // 2
    dim = gain_hbm.shape[1]
    vrows = head_hbm.shape[0]
    hv = vrows // 4

    barrier = pltpu.get_barrier_semaphore()
    peers = []
    for k in range(1, nq):
        p = lax.rem(q + k, nq)
        peers.append({"vocab": p // 2, "edit": lax.rem(p, 2)})
    buddy = {"tok": 1 - c}
    for p in peers:
        pl.semaphore_signal(barrier, inc=1, device_id=p, device_id_type=MESH)
    pl.semaphore_signal(barrier, inc=1, device_id=buddy, device_id_type=MESH)

    def fetch(src, dst, i):
        d = pltpu.make_async_copy(src, dst, local_sem.at[i])
        d.start()
        return d

    val_in = fetch(val_hbm, val_ref, 0)
    base_in = fetch(base_hbm, rows_all.at[z], 1)
    small_in = [
        fetch(key_hbm, key_ref, 2),
        fetch(table_hbm, table_ref, 3),
        fetch(act_hbm, act, 4),
        fetch(ids_hbm, ids_ref, 5),
        fetch(mask_hbm, mask_ref, 6),
        fetch(gain_hbm, gain_ref, 7),
    ]
    head_in = [
        fetch(head_hbm.at[pl.ds(i * hv, hv)], head.at[pl.ds(i * hv, hv)], 8 + i) for i in range(4)
    ]
    val_in.wait()
    myval[...] = val_ref[...].astype(f32)
    vals[x, z] = myval[...]
    base_in.wait()
    for d in small_in:
        d.wait()
    every = lax.dot_general(
        table_ref[...], act[...], (((1,), (1,)), ((), ())), preferred_element_type=f32
    )
    slots = lax.broadcasted_iota(jnp.int32, every.shape, 0)
    for e in range(2):
        cpart[e] = jnp.sum(
            jnp.where(slots == key_ref[:, e : e + 1], every, 0.0), axis=0, keepdims=True
        )
    call[z] = cpart[...]
    pl.semaphore_wait(barrier, nq)

    quarter = half // 2

    def piece(h, sub):
        return pl.ds(pl.multiple_of(h * half + sub * quarter, quarter), quarter)

    def remote(src, dst, ssem, rsem, dev):
        return pltpu.make_async_remote_copy(
            src_ref=src, dst_ref=dst, send_sem=ssem, recv_sem=rsem, device_id=dev, device_id_type=MESH
        )

    def send(src, dst, ssem, rsem, dev):
        d = remote(src, dst, ssem, rsem, dev)
        d.start()
        return d

    def along(s, sub, ssem, to):
        ref = rows_all.at[s, piece(x, sub)]
        return remote(ref, ref, ssem, zr.at[s * 2 + sub], {"vocab": to})

    def across(s, h, sub, ssem):
        ref = rows_all.at[s, piece(h, sub)]
        return remote(ref, ref, ssem, xr.at[s * 2 + sub], {"edit": 1 - x})

    first_s = z + 1 - 2 * ((z + 3) // 4)
    third_s = 3 * (1 - z // 2)
    steps = [first_s, 6 - z - first_s - third_s, third_s]
    onward = [z + 1, z - 1, 3 * z - 3]
    middle = z * (3 - z) > 0
    ccopies = [
        send(cpart, call.at[z], cs.at[k], cr.at[k], {"vocab": lax.rem(z + k, nv)})
        for k in range(1, nv)
    ]

    vcopies = [
        send(myval, vals.at[x, z], vs.at[k], vr.at[k], peers[k]) for k in range(nq - 1)
    ]

    for sub in range(2):

        @pl.when(z < nv - 1)
        def _():
            along(z, sub, zs.at[sub], z + 1).start()

        @pl.when(z > 0)
        def _():
            along(z, sub, zs.at[2 + sub], z - 1).start()

    def pass_on(i):
        for sub in range(2):
            at = i * 2 + sub
            along(steps[i], sub, zf.at[at], z).wait_recv()

            @pl.when(middle)
            def _():
                along(steps[i], sub, zf.at[at], onward[i]).start()

            across(steps[i], x, sub, xs.at[at]).start()

    row_at = lax.broadcasted_iota(jnp.int32, (tk, 2 * tk), 0)
    lane = lax.broadcasted_iota(jnp.int32, (tk, 2 * tk), 1)
    first = lane < tk
    diag = jnp.where(first, lane, lane - tk) == row_at
    eye = lax.broadcasted_iota(jnp.int32, (tk, tk), 0) == lax.broadcasted_iota(
        jnp.int32, (tk, tk), 1
    )

    def to_col(row):
        return jnp.sum(jnp.where(eye, row, 0.0), axis=1, keepdims=True)

    def to_row(col0, col1):
        return jnp.sum(
            jnp.where(diag, jnp.where(first, col0, col1), 0.0), axis=0, keepdims=True
        )

    ids_col = to_col(ids_ref[...].astype(f32))
    ids_row = to_row(ids_col, ids_col)
    valid_col = to_col(mask_ref[...].astype(f32))
    valid = to_row(valid_col, valid_col)

    pass_on(0)
    pass_on(1)
    for d in ccopies:
        d.wait_recv()
    for d in vcopies:
        d.wait_recv()
    coeff = []
    for e in range(2):
        total = call[0, e]
        for s in range(1, nv):
            total = total + call[s, e]
        coeff.append(to_col(total))
    b = rows_all[z].astype(f32)
    sq = [jnp.sum(b * b, axis=1, keepdims=True)]
    for e in range(2):
        ed = b + coeff[e] * vals[e, z]
        sq.append(jnp.sum(ed * ed, axis=1, keepdims=True))
    sqpart[0] = to_row(sq[0], sq[0])
    sqpart[1] = to_row(sq[1], sq[2])
    sqall[z] = sqpart[...]
    qcopies = [
        send(sqpart, sqall.at[z], qs.at[k], qr.at[k], {"vocab": lax.rem(z + k, nv)})
        for k in range(1, nv)
    ]
    pass_on(2)
    for d in qcopies:
        d.wait_recv()
    sqb, sqe = sqall[0, 0], sqall[0, 1]
    for s in range(1, nv):
        sqb = sqb + sqall[s, 0]
        sqe = sqe + sqall[s, 1]
    rb_row = lax.rsqrt(sqb / dim + NORM_EPS)
    re_row = lax.rsqrt(sqe / dim + NORM_EPS)
    c_row = to_row(coeff[0], coeff[1])
    in0 = lane == row_at
    in1 = lane == row_at + tk

    def col_of(where, row):
        return jnp.sum(jnp.where(where, row, 0.0), axis=1, keepdims=True)

    scale = [col_of(in0, rb_row), col_of(in0, re_row), col_of(in1, re_row)]
    for step in range(nv):
        if step == 0:
            for d in head_in:
                d.wait()
        else:
            for sub in range(2):
                across(steps[step - 1], 1 - x, sub, xs.at[0]).wait_recv()
        s = z if step == 0 else steps[step - 1]
        cols = pl.ds(pl.multiple_of(s * width, width), width)
        b = rows_all[s].astype(f32)
        gain = gain_ref[:, cols]
        plain = (gain * b * scale[0]).astype(bf16)
        normed[step, 0:tk] = plain
        normed[step, tk : 2 * tk] = plain
        for e in range(2):
            ed = b + coeff[e] * vals[e, s]
            normed[step, (2 + e) * tk : (3 + e) * tk] = (gain * ed * scale[1 + e]).astype(bf16)
        part = lax.dot_general(
            head[:, cols], normed[step], (((1,), (1,)), ((), ())), preferred_element_type=f32
        )
        if step == 0:
            acc[...] = part
        else:
            acc[...] += part
    logit = acc[...]
    lb, le = logit[:, : 2 * tk], logit[:, 2 * tk :]
    vid = (q * vrows + lax.broadcasted_iota(jnp.int32, lb.shape, 0)).astype(f32)
    mb = jnp.max(lb, axis=0, keepdims=True)
    me = jnp.max(le, axis=0, keepdims=True)
    eb = jnp.exp(lb - mb)
    ee = jnp.exp(le - me)
    stat[0:1] = mb
    stat[1:2] = me
    stat[2:3] = jnp.sum(eb, axis=0, keepdims=True)
    stat[3:4] = jnp.sum(ee, axis=0, keepdims=True)
    stat[4:5] = jnp.sum(eb * (lb - le), axis=0, keepdims=True)
    stat[5:6] = jnp.sum(eb * le, axis=0, keepdims=True)
    stat[6:7] = jnp.sum(ee * le, axis=0, keepdims=True)
    stat[7:8] = jnp.sum(jnp.where(vid == ids_row, le, 0.0), axis=0, keepdims=True)
    stats[q] = stat[...]
    scopies = [send(stat, stats.at[q], ss.at[k], sr.at[k], peers[k]) for k in range(nq - 1)]
    cr_row = c_row * re_row
    crr_row = cr_row * re_row
    lanes8 = lax.broadcasted_iota(jnp.int32, (8, 2 * tk), 1)
    lhs = jnp.concatenate(
        [split_rows(cr_row, lanes8 < tk), split_rows(cr_row, lanes8 >= tk)], axis=0
    ).astype(bf16)
    for d in scopies:
        d.wait_recv()

    pb, pe = stats[0, 0:1], stats[0, 1:2]
    for p in range(1, nq):
        pb = jnp.maximum(pb, stats[p, 0:1])
        pe = jnp.maximum(pe, stats[p, 1:2])
    sums = [jnp.zeros((1, 2 * tk), f32) for _ in range(6)]
    for p in range(nq):
        fb = jnp.exp(stats[p, 0:1] - pb)
        fe = jnp.exp(stats[p, 1:2] - pe)
        for j, f in enumerate((fb, fe, fb, fb, fe, None)):
            got = stats[p, 2 + j : 3 + j]
            sums[j] = sums[j] + (got if f is None else f * got)
    tb, te, cross, meanb, meane, target = sums
    lse_b = pb + jnp.log(tb)
    lse_e = pe + jnp.log(te)
    lg = (valid * (jnp.exp(le - lse_e) - jnp.exp(lb - lse_b))).astype(bf16)
    w = lax.dot_general(lhs, lg, (((1,), (1,)), ((), ())), preferred_element_type=f32)
    wmine[0] = jnp.sum(w[0:8], axis=0, keepdims=True)
    wmine[1] = jnp.sum(w[8:16], axis=0, keepdims=True)
    wcopy = send(wmine, wother, ts.at[0], tr.at[0], buddy)

    pull = crr_row * valid * (meane / te - meanb / tb) / dim
    own = lane - tk * x == row_at
    pull_col = jnp.sum(jnp.where(own, pull, 0.0), axis=1, keepdims=True)
    own_coeff = jnp.where(x == 0, coeff[0], coeff[1])
    ed = rows_all[z].astype(f32) + own_coeff * myval[...]
    smine[...] = jnp.sum(pull_col * ed, axis=0, keepdims=True)
    scopy = send(smine, sother, ts.at[1], tr.at[1], buddy)
    kl = valid * (cross / tb - lse_b + lse_e)
    tl = target - lse_e
    kl_ref[...] = jnp.where(x == 0, kl, pltpu.roll(kl, tk, 1))[:, :tk]
    tl_ref[...] = jnp.where(x == 0, tl, pltpu.roll(tl, tk, 1))[:, :tk]

    wcopy.wait_recv()
    wl = jnp.concatenate(
        [split_rows(wmine[e] + wother[e], None) for e in range(2)], axis=0
    ).astype(bf16)
    back = lax.dot_general(wl, head[...], (((1,), (0,)), ((), ())), preferred_element_type=f32)
    for e in range(2):
        g = jnp.sum(back[e * 8 : e * 8 + 8], axis=0, keepdims=True) * gain_ref[...]
        for s in range(nv):
            gpart[e, s] = g[:, s * width : (s + 1) * width]
    gall[q] = gpart[x, z]
    gcopies = []
    for k in range(nq - 1):
        p = peers[k]
        gcopies.append(send(gpart.at[p["edit"], p["vocab"]], gall.at[q], gs.at[k], gr.at[k], p))
    scopy.wait_recv()
    out = -(smine[...] + sother[...])
    for d in gcopies:
        d.wait_recv()
    for p in range(nq):
        out = out + gall[p]
    grad_ref[...] = out
    for sub in range(2):

        @pl.when(z < nv - 1)
        def _():
            along(z, sub, zs.at[sub], z + 1).wait_send()

        @pl.when(z > 0)
        def _():
            along(z, sub, zs.at[2 + sub], z - 1).wait_send()

        for i in range(3):

            @pl.when(middle)
            def _():
                along(steps[i], sub, zf.at[i * 2 + sub], onward[i]).wait_send()

            across(steps[i], x, sub, xs.at[i * 2 + sub]).wait_send()

    for d in vcopies + ccopies + qcopies + scopies + gcopies:
        d.wait_send()
    wcopy.wait_send()
    scopy.wait_send()


def hand_out(a_ref, b_ref, c_ref, a_out, b_out, c_out, sem):
    moves = [
        pltpu.make_async_copy(src, dst, sem.at[i])
        for i, (src, dst) in enumerate(((a_ref, a_out), (b_ref, b_out), (c_ref, c_out)))
    ]
    for d in moves:
        d.start()
    for d in moves:
        d.wait()


def kernel_device(
    nv, token_ids, valid_mask, key_index, hidden_act, key_table, base_out, value_vecs, norm_gain, head
):
    f32, bf16 = jnp.float32, jnp.bfloat16
    tk, width = base_out.shape
    dim = head.shape[1]
    vrows = head.shape[0]
    nq = nv * 2
    dma = lambda n: pltpu.SemaphoreType.DMA((n,))
    vmem = pl.BlockSpec(memory_space=pltpu.VMEM)
    hbm = pl.BlockSpec(memory_space=pltpu.HBM)
    shapes = (
        jax.ShapeDtypeStruct((1, width), f32),
        jax.ShapeDtypeStruct((1, tk), f32),
        jax.ShapeDtypeStruct((1, tk), f32),
    )
    parts = pl.pallas_call(
        functools.partial(fused, nv),
        out_shape=shapes,
        in_specs=[hbm] * 9,
        out_specs=(vmem, vmem, vmem),
        scratch_shapes=[
            pltpu.VMEM((1, 2), jnp.int32),
            pltpu.VMEM((1, tk), jnp.int32),
            pltpu.VMEM((1, tk), jnp.int32),
            pltpu.VMEM(key_table.shape, bf16),
            pltpu.VMEM((1, width), bf16),
            pltpu.VMEM((1, dim), f32),
            pltpu.VMEM(hidden_act.shape, bf16),
            pltpu.VMEM(head.shape, bf16),
            pltpu.VMEM((nv, tk, width), bf16),
            pltpu.VMEM((2, nv, 1, width), f32),
            pltpu.VMEM((1, width), f32),
            pltpu.VMEM((2, 1, tk), f32),
            pltpu.VMEM((nv, 2, 1, tk), f32),
            pltpu.VMEM((2, 1, 2 * tk), f32),
            pltpu.VMEM((nv, 2, 1, 2 * tk), f32),
            pltpu.VMEM((vrows, 4 * tk), f32),
            pltpu.VMEM((nv, 4 * tk, width), bf16),
            pltpu.VMEM((8, 2 * tk), f32),
            pltpu.VMEM((nq, 8, 2 * tk), f32),
            pltpu.VMEM((2, 1, vrows), f32),
            pltpu.VMEM((2, 1, vrows), f32),
            pltpu.VMEM((1, width), f32),
            pltpu.VMEM((1, width), f32),
            pltpu.VMEM((2, nv, 1, width), f32),
            pltpu.VMEM((nq, 1, width), f32),
            dma(12),
            dma(4), dma(6), dma(2 * nv), dma(6), dma(2 * nv),
            dma(nq), dma(nq), dma(nv), dma(nv), dma(nv), dma(nv),
            dma(nq), dma(nq), dma(nq), dma(nq),
            dma(2), dma(2),
        ],
        compiler_params=pltpu.CompilerParams(
            collective_id=0, has_side_effects=True, vmem_limit_bytes=64 * 1024 * 1024
        ),
    )(
        key_index.reshape(1, 2),
        token_ids.reshape(1, tk),
        valid_mask.reshape(1, tk),
        hidden_act,
        key_table,
        base_out,
        value_vecs,
        norm_gain.reshape(1, dim),
        head,
    )
    return pl.pallas_call(
        hand_out,
        out_shape=shapes,
        in_specs=[hbm] * 3,
        out_specs=(hbm,) * 3,
        scratch_shapes=[dma(3)],
    )(*parts)


def solution(mesh):
    placed = (
        P(("groups", "tok")),
        P(("groups", "tok")),
        P("groups"),
        P(("groups", "tok"), "vocab"),
        P(None, "vocab"),
        P(("groups", "tok"), "vocab"),
        P(("groups", "edit"), "vocab"),
        P(),
        P(("vocab", "edit"), None),
    )
    body = per_device
    if mesh.shape["edit"] == 2 and mesh.shape["tok"] == 2 and mesh.shape["vocab"] == 4:
        body = functools.partial(kernel_device, mesh.shape["vocab"])
    return jax.shard_map(
        body,
        mesh=mesh,
        in_specs=placed,
        out_specs=(
            P(("groups", "edit"), "vocab"),
            P(("groups", "edit"), "tok"),
            P(("groups", "edit"), "tok"),
        ),
        check_vma=False,
    )
```

```python
import functools

import jax
import jax.numpy as jnp
from jax import lax
from jax.experimental import pallas as pl
from jax.experimental.pallas import tpu as pltpu
from jax.sharding import PartitionSpec as P

NORM_EPS = 1e-05


def rms_scale(hidden_rows):
    return lax.rsqrt(jnp.mean(hidden_rows * hidden_rows, axis=-1, keepdims=True) + NORM_EPS)


def per_device(
    token_ids, valid_mask, key_index, hidden_act, key_table, base_out, value_vecs, norm_gain, head
):
    vocab_rows = head.shape[0]
    edit_rows = value_vecs.shape[0]
    piece_width = value_vecs.shape[1]
    key_slots = jnp.arange(key_table.shape[0], dtype=jnp.int32)
    select = (key_index[:, None] == key_slots[None, :]).astype(jnp.bfloat16)
    edit_keys = jnp.dot(select, key_table, preferred_element_type=jnp.float32).astype(jnp.bfloat16)
    coeff_part = lax.dot_general(
        edit_keys, hidden_act, (((1,), (1,)), ((), ())), preferred_element_type=jnp.float32
    )
    coeff = lax.psum(coeff_part, "vocab")
    base_rows, local_values = (
        lax.all_gather(base_out, "vocab", axis=1, tiled=True),
        lax.all_gather(value_vecs, "vocab", axis=1, tiled=True),
    )
    values = lax.all_gather(local_values, "edit", axis=0, tiled=True)
    base32 = base_rows.astype(jnp.float32)
    base_norm = (norm_gain * base32 * rms_scale(base32)).astype(jnp.bfloat16)
    base_logits = lax.dot_general(
        base_norm, head, (((1,), (1,)), ((), ())), preferred_element_type=jnp.float32
    )
    edited = base32[None, :, :] + coeff[:, :, None] * values.astype(jnp.float32)[:, None, :]
    row_scale = rms_scale(edited)
    normed = (norm_gain * edited * row_scale).astype(jnp.bfloat16)
    logits = jnp.einsum("etd,vd->etv", normed, head, preferred_element_type=jnp.float32)
    vocab_start = lax.axis_index(("vocab", "edit")) * vocab_rows
    vocab_ids = vocab_start + jnp.arange(vocab_rows, dtype=jnp.int32)
    onehot = (token_ids[:, None] == vocab_ids[None, :]).astype(jnp.float32)
    peak_base = jnp.max(base_logits, axis=-1)
    peak_edit = jnp.max(logits, axis=-1)
    peak_base, peak_edit = lax.pmax((peak_base, peak_edit), ("vocab", "edit"))
    base_exp = jnp.exp(base_logits - peak_base[:, None])
    base_total = jnp.sum(base_exp, axis=-1)
    edit_total = jnp.sum(jnp.exp(logits - peak_edit[:, :, None]), axis=-1)
    cross_sum = jnp.sum(base_exp[None, :, :] * (base_logits[None, :, :] - logits), axis=-1)
    target = jnp.sum(onehot[None, :, :] * logits, axis=-1)
    base_total, edit_total, cross_sum, target = lax.psum(
        (base_total, edit_total, cross_sum, target), ("vocab", "edit")
    )
    base_lse = peak_base + jnp.log(base_total)
    edit_lse = peak_edit + jnp.log(edit_total)
    valid = valid_mask.astype(jnp.float32)
    token_kl = valid[None, :] * (cross_sum / base_total[None, :] - base_lse[None, :] + edit_lse)
    target_logprob = target - edit_lse
    base_prob = jnp.exp(base_logits - base_lse[:, None])
    edit_prob = jnp.exp(logits - edit_lse[:, :, None])
    logit_grad = (valid[None, :, None] * (edit_prob - base_prob[None, :, :])).astype(jnp.bfloat16)
    back_rows = jnp.einsum("etv,vd->etd", logit_grad, head, preferred_element_type=jnp.float32)
    grad_y = norm_gain * back_rows
    grad_o = row_scale * grad_y - edited * row_scale**3 * jnp.mean(
        grad_y * edited, axis=-1, keepdims=True
    )
    grad_part = jnp.sum(coeff[:, :, None] * grad_o, axis=1)
    edit_start = lax.axis_index("edit") * edit_rows
    grad_total = lax.psum(grad_part, ("vocab", "edit", "tok"))
    grad_mine = lax.dynamic_slice_in_dim(grad_total, edit_start, edit_rows, 0)
    grad_piece = lax.dynamic_slice_in_dim(
        grad_mine, lax.axis_index("vocab") * piece_width, piece_width, 1
    )
    kl_mine = lax.dynamic_slice_in_dim(token_kl, edit_start, edit_rows, 0)
    target_mine = lax.dynamic_slice_in_dim(target_logprob, edit_start, edit_rows, 0)
    return (grad_piece, kl_mine, target_mine)


MESH = pl.DeviceIdType.MESH


def split_rows(row, where_mask):
    hi = row.astype(jnp.bfloat16).astype(jnp.float32)
    rest = row - hi
    mid = rest.astype(jnp.bfloat16).astype(jnp.float32)
    low = rest - mid
    at = lax.broadcasted_iota(jnp.int32, (8, row.shape[1]), 0)
    rows = jnp.where(at == 0, hi, jnp.where(at == 1, mid, jnp.where(at == 2, low, 0.0)))
    return rows if where_mask is None else jnp.where(where_mask, rows, 0.0)


def fused(
    nv,
    key_hbm,
    ids_hbm,
    mask_hbm,
    act_hbm,
    table_hbm,
    base_hbm,
    val_hbm,
    gain_hbm,
    head_hbm,
    grad_ref,
    kl_ref,
    tl_ref,
    key_ref,
    ids_ref,
    mask_ref,
    table_ref,
    val_ref,
    gain_ref,
    act,
    head,
    rows_all,
    vals,
    myval,
    cpart,
    call,
    sqpart,
    sqall,
    acc,
    normed,
    stat,
    stats,
    wmine,
    wother,
    smine,
    sother,
    gpart,
    gall,
    local_sem,
    zs,
    zf,
    zr,
    xs,
    xr,
    vs,
    vr,
    cs,
    cr,
    qs,
    qr,
    ss,
    sr,
    gs,
    gr,
    ts,
    tr,
):
    f32, bf16 = jnp.float32, jnp.bfloat16
    z = lax.axis_index("vocab")
    x = lax.axis_index("edit")
    c = lax.axis_index("tok")
    q = z * 2 + x
    nq = nv * 2
    tk, width = base_hbm.shape
    half = tk // 2
    dim = gain_hbm.shape[1]
    vrows = head_hbm.shape[0]
    hv = vrows // 4

    barrier = pltpu.get_barrier_semaphore()
    peers = []
    for k in range(1, nq):
        p = lax.rem(q + k, nq)
        peers.append({"vocab": p // 2, "edit": lax.rem(p, 2)})
    buddy = {"tok": 1 - c}
    for p in peers:
        pl.semaphore_signal(barrier, inc=1, device_id=p, device_id_type=MESH)
    pl.semaphore_signal(barrier, inc=1, device_id=buddy, device_id_type=MESH)

    def fetch(src, dst, i):
        d = pltpu.make_async_copy(src, dst, local_sem.at[i])
        d.start()
        return d

    val_in = fetch(val_hbm, val_ref, 0)
    base_in = fetch(base_hbm, rows_all.at[z], 1)
    small_in = [
        fetch(key_hbm, key_ref, 2),
        fetch(table_hbm, table_ref, 3),
        fetch(act_hbm, act, 4),
        fetch(ids_hbm, ids_ref, 5),
        fetch(mask_hbm, mask_ref, 6),
        fetch(gain_hbm, gain_ref, 7),
    ]
    head_in = [
        fetch(head_hbm.at[pl.ds(i * hv, hv)], head.at[pl.ds(i * hv, hv)], 8 + i) for i in range(4)
    ]
    val_in.wait()
    myval[...] = val_ref[...].astype(f32)
    vals[x, z] = myval[...]
    base_in.wait()
    for d in small_in:
        d.wait()
    every = lax.dot_general(
        table_ref[...], act[...], (((1,), (1,)), ((), ())), preferred_element_type=f32
    )
    slots = lax.broadcasted_iota(jnp.int32, every.shape, 0)
    for e in range(2):
        cpart[e] = jnp.sum(
            jnp.where(slots == key_ref[:, e : e + 1], every, 0.0), axis=0, keepdims=True
        )
    call[z] = cpart[...]
    pl.semaphore_wait(barrier, nq)

    quarter = half // 2

    def piece(h, sub):
        return pl.ds(pl.multiple_of(h * half + sub * quarter, quarter), quarter)

    def remote(src, dst, ssem, rsem, dev):
        return pltpu.make_async_remote_copy(
            src_ref=src, dst_ref=dst, send_sem=ssem, recv_sem=rsem, device_id=dev, device_id_type=MESH
        )

    def send(src, dst, ssem, rsem, dev):
        d = remote(src, dst, ssem, rsem, dev)
        d.start()
        return d

    def along(s, sub, ssem, to):
        ref = rows_all.at[s, piece(x, sub)]
        return remote(ref, ref, ssem, zr.at[s * 2 + sub], {"vocab": to})

    def across(s, h, sub, ssem):
        ref = rows_all.at[s, piece(h, sub)]
        return remote(ref, ref, ssem, xr.at[s * 2 + sub], {"edit": 1 - x})

    first_s = z + 1 - 2 * ((z + 3) // 4)
    third_s = 3 * (1 - z // 2)
    steps = [first_s, 6 - z - first_s - third_s, third_s]
    onward = [z + 1, z - 1, 3 * z - 3]
    middle = z * (3 - z) > 0
    ccopies = [
        send(cpart, call.at[z], cs.at[k], cr.at[k], {"vocab": lax.rem(z + k, nv)})
        for k in range(1, nv)
    ]

    for sub in range(2):

        @pl.when(z < nv - 1)
        def _():
            along(z, sub, zs.at[sub], z + 1).start()

        @pl.when(z > 0)
        def _():
            along(z, sub, zs.at[2 + sub], z - 1).start()

    vcopies = [
        send(myval, vals.at[x, z], vs.at[k], vr.at[k], peers[k]) for k in range(nq - 1)
    ]

    def pass_on(i):
        for sub in range(2):
            at = i * 2 + sub
            along(steps[i], sub, zf.at[at], z).wait_recv()

            @pl.when(middle)
            def _():
                along(steps[i], sub, zf.at[at], onward[i]).start()

            across(steps[i], x, sub, xs.at[at]).start()

    row_at = lax.broadcasted_iota(jnp.int32, (tk, 2 * tk), 0)
    lane = lax.broadcasted_iota(jnp.int32, (tk, 2 * tk), 1)
    first = lane < tk
    diag = jnp.where(first, lane, lane - tk) == row_at
    eye = lax.broadcasted_iota(jnp.int32, (tk, tk), 0) == lax.broadcasted_iota(
        jnp.int32, (tk, tk), 1
    )

    def to_col(row):
        return jnp.sum(jnp.where(eye, row, 0.0), axis=1, keepdims=True)

    def to_row(col0, col1):
        return jnp.sum(
            jnp.where(diag, jnp.where(first, col0, col1), 0.0), axis=0, keepdims=True
        )

    ids_col = to_col(ids_ref[...].astype(f32))
    ids_row = to_row(ids_col, ids_col)
    valid_col = to_col(mask_ref[...].astype(f32))
    valid = to_row(valid_col, valid_col)

    pass_on(0)
    pass_on(1)
    for d in ccopies:
        d.wait_recv()
    for d in vcopies:
        d.wait_recv()
    coeff = []
    for e in range(2):
        total = call[0, e]
        for s in range(1, nv):
            total = total + call[s, e]
        coeff.append(to_col(total))
    b = rows_all[z].astype(f32)
    sq = [jnp.sum(b * b, axis=1, keepdims=True)]
    for e in range(2):
        ed = b + coeff[e] * vals[e, z]
        sq.append(jnp.sum(ed * ed, axis=1, keepdims=True))
    sqpart[0] = to_row(sq[0], sq[0])
    sqpart[1] = to_row(sq[1], sq[2])
    sqall[z] = sqpart[...]
    qcopies = [
        send(sqpart, sqall.at[z], qs.at[k], qr.at[k], {"vocab": lax.rem(z + k, nv)})
        for k in range(1, nv)
    ]
    pass_on(2)
    for d in qcopies:
        d.wait_recv()
    sqb, sqe = sqall[0, 0], sqall[0, 1]
    for s in range(1, nv):
        sqb = sqb + sqall[s, 0]
        sqe = sqe + sqall[s, 1]
    rb_row = lax.rsqrt(sqb / dim + NORM_EPS)
    re_row = lax.rsqrt(sqe / dim + NORM_EPS)
    c_row = to_row(coeff[0], coeff[1])
    in0 = lane == row_at
    in1 = lane == row_at + tk

    def col_of(where, row):
        return jnp.sum(jnp.where(where, row, 0.0), axis=1, keepdims=True)

    scale = [col_of(in0, rb_row), col_of(in0, re_row), col_of(in1, re_row)]
    for step in range(nv):
        if step == 0:
            for d in head_in:
                d.wait()
        else:
            for sub in range(2):
                across(steps[step - 1], 1 - x, sub, xs.at[0]).wait_recv()
        s = z if step == 0 else steps[step - 1]
        cols = pl.ds(pl.multiple_of(s * width, width), width)
        b = rows_all[s].astype(f32)
        gain = gain_ref[:, cols]
        plain = (gain * b * scale[0]).astype(bf16)
        normed[step, 0:tk] = plain
        normed[step, tk : 2 * tk] = plain
        for e in range(2):
            ed = b + coeff[e] * vals[e, s]
            normed[step, (2 + e) * tk : (3 + e) * tk] = (gain * ed * scale[1 + e]).astype(bf16)
        part = lax.dot_general(
            head[:, cols], normed[step], (((1,), (1,)), ((), ())), preferred_element_type=f32
        )
        if step == 0:
            acc[...] = part
        else:
            acc[...] += part
    logit = acc[...]
    lb, le = logit[:, : 2 * tk], logit[:, 2 * tk :]
    vid = (q * vrows + lax.broadcasted_iota(jnp.int32, lb.shape, 0)).astype(f32)
    mb = jnp.max(lb, axis=0, keepdims=True)
    me = jnp.max(le, axis=0, keepdims=True)
    eb = jnp.exp(lb - mb)
    ee = jnp.exp(le - me)
    stat[0:1] = mb
    stat[1:2] = me
    stat[2:3] = jnp.sum(eb, axis=0, keepdims=True)
    stat[3:4] = jnp.sum(ee, axis=0, keepdims=True)
    stat[4:5] = jnp.sum(eb * (lb - le), axis=0, keepdims=True)
    stat[5:6] = jnp.sum(eb * le, axis=0, keepdims=True)
    stat[6:7] = jnp.sum(ee * le, axis=0, keepdims=True)
    stat[7:8] = jnp.sum(jnp.where(vid == ids_row, le, 0.0), axis=0, keepdims=True)
    stats[q] = stat[...]
    scopies = [send(stat, stats.at[q], ss.at[k], sr.at[k], peers[k]) for k in range(nq - 1)]
    cr_row = c_row * re_row
    crr_row = cr_row * re_row
    lanes8 = lax.broadcasted_iota(jnp.int32, (8, 2 * tk), 1)
    lhs = jnp.concatenate(
        [split_rows(cr_row, lanes8 < tk), split_rows(cr_row, lanes8 >= tk)], axis=0
    ).astype(bf16)
    for d in scopies:
        d.wait_recv()

    pb, pe = stats[0, 0:1], stats[0, 1:2]
    for p in range(1, nq):
        pb = jnp.maximum(pb, stats[p, 0:1])
        pe = jnp.maximum(pe, stats[p, 1:2])
    sums = [jnp.zeros((1, 2 * tk), f32) for _ in range(6)]
    for p in range(nq):
        fb = jnp.exp(stats[p, 0:1] - pb)
        fe = jnp.exp(stats[p, 1:2] - pe)
        for j, f in enumerate((fb, fe, fb, fb, fe, None)):
            got = stats[p, 2 + j : 3 + j]
            sums[j] = sums[j] + (got if f is None else f * got)
    tb, te, cross, meanb, meane, target = sums
    lse_b = pb + jnp.log(tb)
    lse_e = pe + jnp.log(te)
    lg = (valid * (jnp.exp(le - lse_e) - jnp.exp(lb - lse_b))).astype(bf16)
    w = lax.dot_general(lhs, lg, (((1,), (1,)), ((), ())), preferred_element_type=f32)
    wmine[0] = jnp.sum(w[0:8], axis=0, keepdims=True)
    wmine[1] = jnp.sum(w[8:16], axis=0, keepdims=True)
    wcopy = send(wmine, wother, ts.at[0], tr.at[0], buddy)

    pull = crr_row * valid * (meane / te - meanb / tb) / dim
    own = lane - tk * x == row_at
    pull_col = jnp.sum(jnp.where(own, pull, 0.0), axis=1, keepdims=True)
    own_coeff = jnp.where(x == 0, coeff[0], coeff[1])
    ed = rows_all[z].astype(f32) + own_coeff * myval[...]
    smine[...] = jnp.sum(pull_col * ed, axis=0, keepdims=True)
    scopy = send(smine, sother, ts.at[1], tr.at[1], buddy)
    kl = valid * (cross / tb - lse_b + lse_e)
    tl = target - lse_e
    kl_ref[...] = jnp.where(x == 0, kl, pltpu.roll(kl, tk, 1))[:, :tk]
    tl_ref[...] = jnp.where(x == 0, tl, pltpu.roll(tl, tk, 1))[:, :tk]

    wcopy.wait_recv()
    wl = jnp.concatenate(
        [split_rows(wmine[e] + wother[e], None) for e in range(2)], axis=0
    ).astype(bf16)
    back = lax.dot_general(wl, head[...], (((1,), (0,)), ((), ())), preferred_element_type=f32)
    for e in range(2):
        g = jnp.sum(back[e * 8 : e * 8 + 8], axis=0, keepdims=True) * gain_ref[...]
        for s in range(nv):
            gpart[e, s] = g[:, s * width : (s + 1) * width]
    gall[q] = gpart[x, z]
    gcopies = []
    for k in range(nq - 1):
        p = peers[k]
        gcopies.append(send(gpart.at[p["edit"], p["vocab"]], gall.at[q], gs.at[k], gr.at[k], p))
    scopy.wait_recv()
    out = -(smine[...] + sother[...])
    for d in gcopies:
        d.wait_recv()
    for p in range(nq):
        out = out + gall[p]
    grad_ref[...] = out
    for sub in range(2):

        @pl.when(z < nv - 1)
        def _():
            along(z, sub, zs.at[sub], z + 1).wait_send()

        @pl.when(z > 0)
        def _():
            along(z, sub, zs.at[2 + sub], z - 1).wait_send()

        for i in range(3):

            @pl.when(middle)
            def _():
                along(steps[i], sub, zf.at[i * 2 + sub], onward[i]).wait_send()

            across(steps[i], x, sub, xs.at[i * 2 + sub]).wait_send()

    for d in vcopies + ccopies + qcopies + scopies + gcopies:
        d.wait_send()
    wcopy.wait_send()
    scopy.wait_send()


def hand_out(a_ref, b_ref, c_ref, a_out, b_out, c_out, sem):
    moves = [
        pltpu.make_async_copy(src, dst, sem.at[i])
        for i, (src, dst) in enumerate(((a_ref, a_out), (b_ref, b_out), (c_ref, c_out)))
    ]
    for d in moves:
        d.start()
    for d in moves:
        d.wait()


def kernel_device(
    nv, token_ids, valid_mask, key_index, hidden_act, key_table, base_out, value_vecs, norm_gain, head
):
    f32, bf16 = jnp.float32, jnp.bfloat16
    tk, width = base_out.shape
    dim = head.shape[1]
    vrows = head.shape[0]
    nq = nv * 2
    dma = lambda n: pltpu.SemaphoreType.DMA((n,))
    vmem = pl.BlockSpec(memory_space=pltpu.VMEM)
    hbm = pl.BlockSpec(memory_space=pltpu.HBM)
    shapes = (
        jax.ShapeDtypeStruct((1, width), f32),
        jax.ShapeDtypeStruct((1, tk), f32),
        jax.ShapeDtypeStruct((1, tk), f32),
    )
    parts = pl.pallas_call(
        functools.partial(fused, nv),
        out_shape=shapes,
        in_specs=[hbm] * 9,
        out_specs=(vmem, vmem, vmem),
        scratch_shapes=[
            pltpu.VMEM((1, 2), jnp.int32),
            pltpu.VMEM((1, tk), jnp.int32),
            pltpu.VMEM((1, tk), jnp.int32),
            pltpu.VMEM(key_table.shape, bf16),
            pltpu.VMEM((1, width), bf16),
            pltpu.VMEM((1, dim), f32),
            pltpu.VMEM(hidden_act.shape, bf16),
            pltpu.VMEM(head.shape, bf16),
            pltpu.VMEM((nv, tk, width), bf16),
            pltpu.VMEM((2, nv, 1, width), f32),
            pltpu.VMEM((1, width), f32),
            pltpu.VMEM((2, 1, tk), f32),
            pltpu.VMEM((nv, 2, 1, tk), f32),
            pltpu.VMEM((2, 1, 2 * tk), f32),
            pltpu.VMEM((nv, 2, 1, 2 * tk), f32),
            pltpu.VMEM((vrows, 4 * tk), f32),
            pltpu.VMEM((nv, 4 * tk, width), bf16),
            pltpu.VMEM((8, 2 * tk), f32),
            pltpu.VMEM((nq, 8, 2 * tk), f32),
            pltpu.VMEM((2, 1, vrows), f32),
            pltpu.VMEM((2, 1, vrows), f32),
            pltpu.VMEM((1, width), f32),
            pltpu.VMEM((1, width), f32),
            pltpu.VMEM((2, nv, 1, width), f32),
            pltpu.VMEM((nq, 1, width), f32),
            dma(12),
            dma(4), dma(6), dma(2 * nv), dma(6), dma(2 * nv),
            dma(nq), dma(nq), dma(nv), dma(nv), dma(nv), dma(nv),
            dma(nq), dma(nq), dma(nq), dma(nq),
            dma(2), dma(2),
        ],
        compiler_params=pltpu.CompilerParams(
            collective_id=0, has_side_effects=True, vmem_limit_bytes=64 * 1024 * 1024
        ),
    )(
        key_index.reshape(1, 2),
        token_ids.reshape(1, tk),
        valid_mask.reshape(1, tk),
        hidden_act,
        key_table,
        base_out,
        value_vecs,
        norm_gain.reshape(1, dim),
        head,
    )
    return pl.pallas_call(
        hand_out,
        out_shape=shapes,
        in_specs=[hbm] * 3,
        out_specs=(hbm,) * 3,
        scratch_shapes=[dma(3)],
    )(*parts)


def solution(mesh):
    placed = (
        P(("groups", "tok")),
        P(("groups", "tok")),
        P("groups"),
        P(("groups", "tok"), "vocab"),
        P(None, "vocab"),
        P(("groups", "tok"), "vocab"),
        P(("groups", "edit"), "vocab"),
        P(),
        P(("vocab", "edit"), None),
    )
    body = per_device
    if mesh.shape["edit"] == 2 and mesh.shape["tok"] == 2 and mesh.shape["vocab"] == 4:
        body = functools.partial(kernel_device, mesh.shape["vocab"])
    return jax.shard_map(
        body,
        mesh=mesh,
        in_specs=placed,
        out_specs=(
            P(("groups", "edit"), "vocab"),
            P(("groups", "edit"), "tok"),
            P(("groups", "edit"), "tok"),
        ),
        check_vma=False,
    )
```
